256 devices in a mesh: replica: 32 (over x, z_lo, y), fsdp: 8 (over z_hi, core).
Axes of the slice: x: 4, y: 4, z: 8 (z_hi: 4, z_lo: 2; z = z_hi * 2 + z_lo), core: 2. Of those that a mesh axis runs over, the one named last changes fastest.
Arguments:
- tokens: bfloat16 [131072, 4096], P(('replica', 'fsdp')), may hold values from -6 to 6
- key_cotangent: bfloat16 [131072, 512], P(('replica', 'fsdp')), may hold values from -0.1875 to 0.1875
- key_weight: bfloat16 [131072, 512], P(('replica', 'fsdp')), may hold values from -0.09375 to 0.09375
- first_moment: float32 [131072, 512], P(('replica', 'fsdp')), may hold values from -6 to 6
- second_moment: float32 [131072, 512], P(('replica', 'fsdp')), may hold values from 0.1 to 3
- local_slab: bfloat16 [49152, 4096], P(('replica', 'fsdp')), as said below
- outer_params: float32 [1536, 4096], P('fsdp', 'replica')
- outer_momentum: float32 [1536, 4096], P('fsdp', 'replica'), may hold values from -3 to 3
Outputs:
- projected: bfloat16 [131072, 512], P(('replica', 'fsdp'))
- new_weight: bfloat16 [131072, 512], P(('replica', 'fsdp'))
- new_first: float32 [131072, 512], P(('replica', 'fsdp'))
- new_second: float32 [131072, 512], P(('replica', 'fsdp'))
- new_outer: float32 [1536, 4096], P('fsdp', 'replica')
- new_momentum: float32 [1536, 4096], P('fsdp', 'replica')
- new_local: bfloat16 [49152, 4096], P(('replica', 'fsdp'))
The draws below stay inside these ranges and needn't reach their ends.
Inputs may be any that keep to these rules, and one draw needn't show every extreme that they name: `local_slab`: each replica's fragment equals outer_params plus a drift that the replicas partly share.
All inputs are finite; a program needn't handle non-finite values.
Results may differ from the reference program's by a relative error of at most 0.00045.
Values may be sent and summed in bfloat16 or wider, within the bound.
A program may use at most 128 MiB of HBM per device.

```python
import math
import jax
import jax.numpy as jnp
from jax import lax

D = 4096
KEY_WIDTH = 512
REPLICAS = 32
REP_TOKENS = 4096
TOKENS = 131072
FRAG = 1536


def shared_base(key):
    return jax.random.normal(jax.random.fold_in(key, 11), (FRAG, D), jnp.float32)


def draw_outer_params(key, part):
    return shared_base(key)


def draw_local_slab(key, part):
    base = shared_base(key)
    common = 0.5 * jax.random.normal(jax.random.fold_in(key, 12), (FRAG, D), jnp.float32)
    spread = 0.3 * jax.random.normal(jax.random.fold_in(key, 13), (REPLICAS, FRAG, D), jnp.float32)
    slabs = base[None] + common[None] + spread
    return slabs.reshape(REPLICAS * FRAG, D).astype(jnp.bfloat16)


def block_scale(own_key, dims, split, smallest, largest):
    level, own = 1.0, jax.random.fold_in(own_key, 6)
    for dim, shards_of in split:
        steps = jnp.exp(jax.random.uniform(jax.random.fold_in(own, dim), (shards_of,), jnp.float32, smallest / len(split), largest / len(split)))
        level = level * jnp.repeat(steps, dims[dim] // shards_of).reshape([-1 if axis == dim else 1 for axis in range(len(dims))])
    return level


def normal_values(stream_key, dims, deviation, bound, split=(), kind=jnp.bfloat16):
    entries = jax.random.normal(stream_key, dims, jnp.float32) * deviation
    if len(split) > 0:
        entries = block_scale(stream_key, dims, split, -0.22, 0.18) * entries
    return jnp.clip(entries, min=-bound, max=bound).astype(kind)


def setup_inputs(seed: int = 0) -> dict:
    splits = jax.random.split(jax.random.key(seed), 9)
    tokens = normal_values(splits[0], (TOKENS, D), 1.0, 6.0, ((0, 256),))
    key_cotangent = normal_values(splits[1], (TOKENS, KEY_WIDTH), (REP_TOKENS // 4) ** -0.5, 0.1875, ((0, 256),))
    key_weight = normal_values(splits[2], (REPLICAS * D, KEY_WIDTH), D ** -0.5, 0.09375, ((0, 256),))
    first_moment = normal_values(splits[3], (REPLICAS * D, KEY_WIDTH), 1.0, 6.0, ((0, 256),), jnp.float32)
    second_moment = jnp.clip(jnp.exp(math.log(3.0) - 3.4011974 * jax.random.uniform(splits[4], (REPLICAS * D, KEY_WIDTH), jnp.float32) ** block_scale(splits[4], (REPLICAS * D, KEY_WIDTH), ((0, 256),), -0.2, 0.2)), 0.1, 3.0)
    local_slab = draw_local_slab(jax.random.fold_in(splits[8], 71), 0)
    outer_params = draw_outer_params(jax.random.fold_in(splits[8], 71), 0)
    outer_momentum = normal_values(splits[7], (FRAG, D), 0.5, 3.0, ((0, 8), (1, 32)), jnp.float32)
    return dict(tokens=tokens, key_cotangent=key_cotangent, key_weight=key_weight, first_moment=first_moment, second_moment=second_moment, local_slab=local_slab, outer_params=outer_params, outer_momentum=outer_momentum)


BETA_ONE = 0.9
BETA_TWO = 0.95
INNER_RATE = 0.001
DECAY_RATE = 0.1
EPSILON = 1e-08
FIRST_FIX = 1.0 - (0.9 ** 50) ** 2
SECOND_FIX = 1.0 - (0.95 ** 50) ** 2
OUTER_RATE = 0.7
OUTER_MOMENTUM = 0.9
MERGE_WEIGHT = 0.5

def reference(tokens, key_cotangent, key_weight, first_moment, second_moment, local_slab, outer_params, outer_momentum):
    rep_tokens = tokens.reshape(REPLICAS, REP_TOKENS, D)
    rep_cot = key_cotangent.reshape(REPLICAS, REP_TOKENS, KEY_WIDTH)
    rep_weight = key_weight.reshape(REPLICAS, D, KEY_WIDTH)

    def one_replica(index):
        inputs = rep_tokens[index]
        keyed = jnp.dot(inputs, rep_weight[index], preferred_element_type=jnp.float32).astype(jnp.bfloat16)
        gradient = lax.dot_general(inputs, rep_cot[index], (((0,), (0,)), ((), ())), preferred_element_type=jnp.float32)
        return (keyed, gradient)
    projected, gradient = lax.map(one_replica, jnp.arange(REPLICAS, dtype=jnp.int32))
    projected = projected.reshape(TOKENS, KEY_WIDTH)
    gradient = gradient.reshape(REPLICAS * D, KEY_WIDTH)
    new_first = BETA_ONE * first_moment + (1.0 - BETA_ONE) * gradient
    new_second = BETA_TWO * second_moment + (1.0 - BETA_TWO) * gradient * gradient
    weight_f = key_weight.astype(jnp.float32)
    update = new_first / FIRST_FIX / (jnp.sqrt(new_second / SECOND_FIX) + EPSILON) + DECAY_RATE * weight_f
    new_weight = (weight_f - INNER_RATE * update).astype(jnp.bfloat16)
    slabs = local_slab.reshape(REPLICAS, FRAG, D).astype(jnp.float32)
    average = lax.optimization_barrier(jnp.sum(slabs, axis=0)) / REPLICAS
    pseudo_grad = outer_params - average
    new_momentum = OUTER_MOMENTUM * outer_momentum + pseudo_grad
    new_outer = outer_params - OUTER_RATE * (pseudo_grad + OUTER_MOMENTUM * new_momentum)
    merged = MERGE_WEIGHT * slabs + (1.0 - MERGE_WEIGHT) * new_outer[None]
    new_local = merged.astype(jnp.bfloat16).reshape(REPLICAS * FRAG, D)
    return (projected, new_weight, new_first, new_second, new_outer, new_momentum, new_local)
```

```python
import jax
import jax.numpy as jnp
from jax import lax
from jax.experimental import pallas as pl
from jax.experimental.pallas import tpu as pltpu
from jax.sharding import PartitionSpec as P

BETA_ONE = 0.9
BETA_TWO = 0.95
INNER_RATE = 0.001
DECAY_RATE = 0.1
EPSILON = 1e-08
FIRST_FIX = 1.0 - (0.9**50) ** 2
SECOND_FIX = 1.0 - (0.95**50) ** 2
OUTER_RATE = 0.7
OUTER_MOMENTUM = 0.9
MERGE_WEIGHT = 0.5

MESH = pl.DeviceIdType.MESH
F32, BF16 = jnp.float32, jnp.bfloat16
B = 512
HB = 256
ROWS = 192
HR = 96
LANES = 128
REPLICAS = 32

W_UP, W_DOWN, W_CORE, W_UP2, W_DOWN2, W_CORE_UP, W_CORE_DOWN, W_CORE_FAR = range(8)
X_CORE = 8
C_CORE = 12
G_UP1, G_DOWN1, G_UP, G_DOWN, G_UP2, G_DOWN2 = range(13, 19)
RS_A0, RS_A1, RS_B0, RS_B1 = 19, 22, 25, 28
RS_Z = 31
AG_Z = 32
AG_A0, AG_A1, AG_B0, AG_B1 = 33, 36, 39, 42
W_CORE_FAR2 = 45
N_REMOTE = 46


def kernel(
    tok_ref, cot_ref, w_ref, first_ref, second_ref, slab_ref, outer_ref, mom_ref,
    proj_out, neww_out, first_out, second_out, outer_out, mom_out, local_out,
    xb, xo, cb, co, wb, g, r1, ru, ra, m1, m2,
    slab, ra0, ra1, pa0, pa1, rb0, rb1, tb, rz, po, pm, agb, nl,
    acc, pj, nw,
    ss, rs, ls, xs, slab_s, os,
):
    r = lax.axis_index("replica")
    f = lax.axis_index("fsdp")
    x, zl, y = lax.div(r, 8), lax.rem(lax.div(r, 4), 2), lax.rem(r, 4)
    zh, c = lax.div(f, 2), lax.rem(f, 2)

    def turn(value, step, size=4):
        return lax.rem(value + step + size, size)

    def dev(x_, zl_, y_, zh_, c_):
        return {"replica": (x_ * 2 + zl_) * 4 + y_, "fsdp": zh_ * 2 + c_}

    def at_x(d):
        return dev(turn(x, d), zl, y, zh, c)

    def at_y(d):
        return dev(x, zl, turn(y, d), zh, c)

    up, down = dev(x, zl, y, turn(zh, 1), c), dev(x, zl, y, turn(zh, -1), c)
    pair = dev(x, 1 - zl, y, zh, c)
    core = dev(x, zl, y, zh, 1 - c)

    def remote(place, src, dst, device):
        return pltpu.make_async_remote_copy(
            src_ref=src, dst_ref=dst, send_sem=ss.at[place], recv_sem=rs.at[place],
            device_id=device, device_id_type=MESH,
        )

    sent = []

    def send(place, src, dst, device):
        copy = remote(place, src, dst, device)
        copy.start()
        sent.append(copy)
        return copy

    def rows(total, step, body):
        def one(i, _):
            body(pl.ds(pl.multiple_of(i * step, step), step))
            return 0
        lax.fori_loop(0, total // step, one, 0)

    own_w = pltpu.make_async_copy(w_ref, wb.at[f], ls.at[0])
    own_w.start()
    own_c = pltpu.make_async_copy(cot_ref, cb, ls.at[1])
    own_c.start()
    own_x = []
    for k in range(8):
        copy = pltpu.make_async_copy(tok_ref.at[:, k * B:(k + 1) * B], xb.at[k], xs.at[k])
        copy.start()
        own_x.append(copy)

    def slab_copy(k):
        return pltpu.make_async_copy(
            slab_ref.at[:, k * LANES:(k + 1) * LANES], slab.at[k // 4, k % 4], slab_s.at[k]
        )
    for k in range(32):
        slab_copy(k).start()
    own_m1 = pltpu.make_async_copy(first_ref, m1, ls.at[2])
    own_m2 = pltpu.make_async_copy(second_ref, m2, ls.at[3])
    own_po = pltpu.make_async_copy(outer_ref, po, ls.at[4])
    own_pm = pltpu.make_async_copy(mom_ref, pm, ls.at[5])
    for copy in (own_po, own_pm, own_m1, own_m2):
        copy.start()

    barrier = pltpu.get_barrier_semaphore()
    partners = [up, down, core, pair] + [at_x(d) for d in (1, 2, 3)] + [at_y(d) for d in (1, 2, 3)]
    for partner in partners:
        pl.semaphore_signal(barrier, inc=1, device_id=partner, device_id_type=MESH)
    pl.semaphore_wait(barrier, len(partners))

    own_w.wait()
    w_up = send(W_UP, wb.at[f], wb.at[f], up)
    w_down = send(W_DOWN, wb.at[f], wb.at[f], down)
    w_core = send(W_CORE, wb.at[f], wb.at[f], core)

    own_c.wait()
    c_core = send(C_CORE, cb, co, core)
    for copy in own_x:
        copy.wait()
    x_core = {}
    for d in (2, 1, 3, 0):
        x_core[d] = send(X_CORE + d, xb.at[2 * turn(zh, d) + 1 - c], xo.at[d], core)

    for k in range(32):
        slab_copy(k).wait()
    a0, a1 = [], []
    for d in (1, 2, 3):
        a0.append(send(RS_A0 + d - 1, slab.at[pl.ds(2 * turn(x, d), 2), :, 0:HR], ra0.at[d - 1], at_x(d)))
        a1.append(send(RS_A1 + d - 1, slab.at[:, turn(y, d), HR:ROWS], ra1.at[d - 1], at_y(d)))

    def gradient(d):
        x_core[d].wait_recv()
        dims = (((0,), (0,)), ((), ()))
        mine = lax.dot_general(xb[2 * turn(zh, d) + c], cb[...], dims, preferred_element_type=F32)
        g[d] = mine
        other = lax.dot_general(xo[d], co[...], dims, preferred_element_type=F32)
        g[d] += other

    c_core.wait_recv()
    gradient(2)
    g_up1 = send(G_UP1, g.at[2, 0:HB], r1.at[0], up)
    g_down1 = send(G_DOWN1, g.at[2, HB:B], r1.at[1], down)
    gradient(1)
    g_up = send(G_UP, g.at[1, HB:B], ru.at[0], up)
    gradient(3)
    g_down = send(G_DOWN, g.at[3, 0:HB], ru.at[1], down)
    gradient(0)

    def project(k, start=False):
        part = jnp.dot(xb[k], wb[k], preferred_element_type=F32)
        if start:
            acc[...] = part
        else:
            acc[...] += part

    project(f, True)

    for copy in a0:
        copy.wait_recv()
    for kk in range(2):
        for yy in range(4):
            pa0[kk, yy] = (
                slab[2 * x + kk, yy, 0:HR].astype(F32) + ra0[0, kk, yy].astype(F32)
                + ra0[1, kk, yy].astype(F32) + ra0[2, kk, yy].astype(F32)
            )
    b0 = [send(RS_B0 + d - 1, pa0.at[:, turn(y, d)], rb0.at[d - 1], at_y(d)) for d in (1, 2, 3)]
    for copy in a1:
        copy.wait_recv()
    for k in range(8):
        pa1[k] = (
            slab[k, y, HR:ROWS].astype(F32) + ra1[0, k].astype(F32)
            + ra1[1, k].astype(F32) + ra1[2, k].astype(F32)
        )
    b1 = [send(RS_B1 + d - 1, pa1.at[pl.ds(2 * turn(x, d), 2)], rb1.at[d - 1], at_x(d)) for d in (1, 2, 3)]
    for copy in b0:
        copy.wait_recv()
    for copy in b1:
        copy.wait_recv()
    for kk in range(2):
        tb[kk, 0:HR] = pa0[kk, y] + rb0[0, kk] + rb0[1, kk] + rb0[2, kk]
        tb[kk, HR:ROWS] = pa1[2 * x + kk] + rb1[0, kk] + rb1[1, kk] + rb1[2, kk]
    z_sum = send(RS_Z, tb.at[1 - zl], rz, pair)

    w_core.wait_recv()
    project(2 * zh + 1 - c)

    w_up.wait_recv()
    below = 2 * turn(zh, -1) + c
    w_up2 = send(W_UP2, wb.at[below, 0:HB], wb.at[below, 0:HB], up)
    w_core_up = send(W_CORE_UP, wb.at[below], wb.at[below], core)
    w_down.wait_recv()
    above = 2 * turn(zh, 1) + c
    w_down2 = send(W_DOWN2, wb.at[above, HB:B], wb.at[above, HB:B], down)
    w_core_down = send(W_CORE_DOWN, wb.at[above], wb.at[above], core)

    z_sum.wait_recv()
    own_po.wait()
    own_pm.wait()
    average = (tb[zl] + rz[...]) / REPLICAS
    pseudo_grad = po[...] - average
    new_momentum = OUTER_MOMENTUM * pm[...] + pseudo_grad
    new_outer = po[...] - OUTER_RATE * (pseudo_grad + OUTER_MOMENTUM * new_momentum)
    pm[...] = new_momentum
    agb[2 * x + zl, y] = new_outer
    outs = []

    def put(place, src, dst):
        copy = pltpu.make_async_copy(src, dst, os.at[place])
        copy.start()
        outs.append(copy)

    z_gather = send(AG_Z, agb.at[2 * x + zl, y], agb.at[2 * x + zl, y], pair)
    put(0, pm, mom_out)
    put(1, agb.at[2 * x + zl, y], outer_out)

    g_up1.wait_recv()
    g[1, 0:HB] += r1[0]
    g_up2 = send(G_UP2, g.at[1, 0:HB], ra.at[0], up)
    g_down1.wait_recv()
    g[3, HB:B] += r1[1]
    g_down2 = send(G_DOWN2, g.at[3, HB:B], ra.at[1], down)

    z_gather.wait_recv()
    g0 = [send(AG_A0 + d - 1, agb.at[pl.ds(2 * x, 2), y, 0:HR], agb.at[pl.ds(2 * x, 2), y, 0:HR], at_x(d)) for d in (1, 2, 3)]
    g1 = [send(AG_A1 + d - 1, agb.at[pl.ds(2 * x, 2), y, HR:ROWS], agb.at[pl.ds(2 * x, 2), y, HR:ROWS], at_y(d)) for d in (1, 2, 3)]
    w_core_up.wait_recv()
    w_core_down.wait_recv()
    for s in (-1, 1):
        project(2 * turn(zh, s) + c)
        project(2 * turn(zh, s) + 1 - c)
    for copy in g0:
        copy.wait_recv()
    h0 = [send(AG_B0 + d - 1, agb.at[:, y, 0:HR], agb.at[:, y, 0:HR], at_y(d)) for d in (1, 2, 3)]
    for copy in g1:
        copy.wait_recv()
    h1 = [send(AG_B1 + d - 1, agb.at[pl.ds(2 * x, 2), :, HR:ROWS], agb.at[pl.ds(2 * x, 2), :, HR:ROWS], at_x(d)) for d in (1, 2, 3)]

    g_up.wait_recv()
    g[0, HB:B] += ru[0]
    g_down.wait_recv()
    g[0, 0:HB] += ru[1]

    for copy in h0:
        copy.wait_recv()
    for copy in h1:
        copy.wait_recv()
    for k in range(32):
        block = MERGE_WEIGHT * slab[k // 4, k % 4].astype(F32) + (1.0 - MERGE_WEIGHT) * agb[k // 4, k % 4]
        nl[:, k * LANES:(k + 1) * LANES] = block.astype(BF16)
    put(2, nl, local_out)

    far = 2 * turn(zh, 2) + c
    w_up2.wait_recv()
    w_far = send(W_CORE_FAR, wb.at[far, 0:HB], wb.at[far, 0:HB], core)
    w_down2.wait_recv()
    w_far2 = send(W_CORE_FAR2, wb.at[far, HB:B], wb.at[far, HB:B], core)
    project(far)
    w_far.wait_recv()
    w_far2.wait_recv()
    project(2 * turn(zh, 2) + 1 - c)
    pj[...] = acc[...].astype(BF16)
    put(3, pj, proj_out)

    own_m1.wait()
    own_m2.wait()

    def adam(part, half):
        def body(at):
            grad = g[0, at] + ra[half, pl.ds(at.start - half * HB, at.size)]
            new_first = BETA_ONE * m1[at] + (1.0 - BETA_ONE) * grad
            new_second = BETA_TWO * m2[at] + (1.0 - BETA_TWO) * grad * grad
            weight = wb[f, at].astype(F32)
            update = new_first / FIRST_FIX / (jnp.sqrt(new_second / SECOND_FIX) + EPSILON) + DECAY_RATE * weight
            m1[at] = new_first
            m2[at] = new_second
            nw[at] = (weight - INNER_RATE * update).astype(BF16)

        def one(i, _):
            body(pl.ds(pl.multiple_of(half * HB + i * 32, 32), 32))
            return 0
        lax.fori_loop(0, HB // 32, one, 0)

    g_up2.wait_recv()
    adam(g_up2, 0)
    g_down2.wait_recv()
    adam(g_down2, 1)
    put(4, m1, first_out)
    put(5, m2, second_out)
    put(6, nw, neww_out)
    for copy in sent:
        copy.wait_send()
    for copy in outs:
        copy.wait()


def shards(tokens, key_cotangent, key_weight, first_moment, second_moment, local_slab, outer_params, outer_momentum):
    out_shape = (
        jax.ShapeDtypeStruct((B, B), BF16),
        jax.ShapeDtypeStruct((B, B), BF16),
        jax.ShapeDtypeStruct((B, B), F32),
        jax.ShapeDtypeStruct((B, B), F32),
        jax.ShapeDtypeStruct((ROWS, LANES), F32),
        jax.ShapeDtypeStruct((ROWS, LANES), F32),
        jax.ShapeDtypeStruct((ROWS, 4096), BF16),
    )
    vmem = pltpu.VMEM
    return pl.pallas_call(
        kernel,
        out_shape=out_shape,
        in_specs=[pl.BlockSpec(memory_space=pl.ANY)] * 8,
        out_specs=(pl.BlockSpec(memory_space=pl.ANY),) * 7,
        scratch_shapes=[
            vmem((8, B, B), BF16),
            vmem((4, B, B), BF16),
            vmem((B, B), BF16),
            vmem((B, B), BF16),
            vmem((8, B, B), BF16),
            vmem((4, B, B), F32),
            vmem((2, HB, B), F32),
            vmem((2, HB, B), F32),
            vmem((2, HB, B), F32),
            vmem((B, B), F32),
            vmem((B, B), F32),
            vmem((8, 4, ROWS, LANES), BF16),
            vmem((3, 2, 4, HR, LANES), BF16),
            vmem((3, 8, HR, LANES), BF16),
            vmem((2, 4, HR, LANES), F32),
            vmem((8, HR, LANES), F32),
            vmem((3, 2, HR, LANES), F32),
            vmem((3, 2, HR, LANES), F32),
            vmem((2, ROWS, LANES), F32),
            vmem((ROWS, LANES), F32),
            vmem((ROWS, LANES), F32),
            vmem((ROWS, LANES), F32),
            vmem((8, 4, ROWS, LANES), F32),
            vmem((ROWS, 4096), BF16),
            vmem((B, B), F32),
            vmem((B, B), BF16),
            vmem((B, B), BF16),
            pltpu.SemaphoreType.DMA((N_REMOTE,)),
            pltpu.SemaphoreType.DMA((N_REMOTE,)),
            pltpu.SemaphoreType.DMA((6,)),
            pltpu.SemaphoreType.DMA((8,)),
            pltpu.SemaphoreType.DMA((32,)),
            pltpu.SemaphoreType.DMA((7,)),
        ],
        name="window",
        compiler_params=pltpu.CompilerParams(
            collective_id=0, has_side_effects=True, vmem_limit_bytes=48 << 20
        ),
    )(tokens, key_cotangent, key_weight, first_moment, second_moment, local_slab, outer_params, outer_momentum)


def solution(mesh):
    both = P(("replica", "fsdp"), None)
    cut = P("fsdp", "replica")
    return jax.shard_map(
        shards,
        mesh=mesh,
        in_specs=(both, both, both, both, both, both, cut, cut),
        out_specs=(both, both, both, both, cut, cut, both),
        check_vma=False,
    )
```

```python
import jax
import jax.numpy as jnp
from jax import lax
from jax.experimental import pallas as pl
from jax.experimental.pallas import tpu as pltpu
from jax.sharding import PartitionSpec as P

BETA_ONE = 0.9
BETA_TWO = 0.95
INNER_RATE = 0.001
DECAY_RATE = 0.1
EPSILON = 1e-08
FIRST_FIX = 1.0 - (0.9**50) ** 2
SECOND_FIX = 1.0 - (0.95**50) ** 2
OUTER_RATE = 0.7
OUTER_MOMENTUM = 0.9
MERGE_WEIGHT = 0.5

MESH = pl.DeviceIdType.MESH
F32, BF16 = jnp.float32, jnp.bfloat16
B = 512
HB = 256
ROWS = 192
HR = 96
LANES = 128
REPLICAS = 32

W_UP, W_DOWN, W_CORE, W_UP2, W_DOWN2, W_CORE_UP, W_CORE_DOWN, W_CORE_FAR = range(8)
X_CORE = 8
C_CORE = 12
G_UP1, G_DOWN1, G_UP, G_DOWN, G_UP2, G_DOWN2 = range(13, 19)
RS_A0, RS_A1, RS_B0, RS_B1 = 19, 22, 25, 28
RS_Z = 31
AG_Z = 32
AG_A0, AG_A1, AG_B0, AG_B1 = 33, 36, 39, 42
W_CORE_FAR2 = 45
N_REMOTE = 46


def packed(v):
    t = 8.0 * v
    t2 = t * t
    t4 = t2 * t2
    t8 = t4 * t4
    return jnp.where(v < 0.0, -t8, t8).astype(BF16)


def unpacked(p):
    p = p.astype(F32)
    v = 0.125 * jnp.sqrt(jnp.sqrt(jnp.sqrt(jnp.abs(p))))
    return jnp.where(p < 0.0, -v, v)


def kernel(
    tok_ref, cot_ref, w_ref, first_ref, second_ref, slab_ref, outer_ref, mom_ref,
    proj_out, neww_out, first_out, second_out, outer_out, mom_out, local_out,
    xb, xo, cb, co, wb, g, sb, r1, ru, ra, m1, m2,
    slab, ra0, ra1, pa0, pa1, rb0, rb1, tb, rz, po, pm, agb, acc,
    ss, rs, ls, xs, slab_s,
):
    r = lax.axis_index("replica")
    f = lax.axis_index("fsdp")
    x, zl, y = lax.div(r, 8), lax.rem(lax.div(r, 4), 2), lax.rem(r, 4)
    zh, c = lax.div(f, 2), lax.rem(f, 2)

    def turn(value, step, size=4):
        return lax.rem(value + step + size, size)

    def dev(x_, zl_, y_, zh_, c_):
        return {"replica": (x_ * 2 + zl_) * 4 + y_, "fsdp": zh_ * 2 + c_}

    def at_x(d):
        return dev(turn(x, d), zl, y, zh, c)

    def at_y(d):
        return dev(x, zl, turn(y, d), zh, c)

    up, down = dev(x, zl, y, turn(zh, 1), c), dev(x, zl, y, turn(zh, -1), c)
    pair = dev(x, 1 - zl, y, zh, c)
    core = dev(x, zl, y, zh, 1 - c)

    def remote(place, src, dst, device):
        return pltpu.make_async_remote_copy(
            src_ref=src, dst_ref=dst, send_sem=ss.at[place], recv_sem=rs.at[place],
            device_id=device, device_id_type=MESH,
        )

    sent = []

    def send(place, src, dst, device):
        copy = remote(place, src, dst, device)
        copy.start()
        sent.append(copy)
        return copy

    def rows(total, step, body):
        def one(i, _):
            body(pl.ds(pl.multiple_of(i * step, step), step))
            return 0
        lax.fori_loop(0, total // step, one, 0)

    own_w = pltpu.make_async_copy(w_ref, wb.at[f], ls.at[0])
    own_w.start()
    own_c = pltpu.make_async_copy(cot_ref, cb, ls.at[1])
    own_c.start()
    own_x = []
    for k in range(8):
        copy = pltpu.make_async_copy(tok_ref.at[:, k * B:(k + 1) * B], xb.at[k], xs.at[k])
        copy.start()
        own_x.append(copy)

    def slab_copy(k):
        return pltpu.make_async_copy(
            slab_ref.at[:, k * LANES:(k + 1) * LANES], slab.at[k // 4, k % 4], slab_s.at[k]
        )
    for k in range(32):
        slab_copy(k).start()
    own_m1 = pltpu.make_async_copy(first_ref, m1, ls.at[2])
    own_m2 = pltpu.make_async_copy(second_ref, m2, ls.at[3])
    own_po = pltpu.make_async_copy(outer_ref, po, ls.at[4])
    own_pm = pltpu.make_async_copy(mom_ref, pm, ls.at[5])
    for copy in (own_po, own_pm, own_m1, own_m2):
        copy.start()

    barrier = pltpu.get_barrier_semaphore()
    partners = [up, down, core, pair] + [at_x(d) for d in (1, 2, 3)] + [at_y(d) for d in (1, 2, 3)]
    for partner in partners:
        pl.semaphore_signal(barrier, inc=1, device_id=partner, device_id_type=MESH)
    pl.semaphore_wait(barrier, len(partners))

    own_w.wait()
    w_up = send(W_UP, wb.at[f], wb.at[f], up)
    w_down = send(W_DOWN, wb.at[f], wb.at[f], down)
    w_core = send(W_CORE, wb.at[f], wb.at[f], core)

    own_c.wait()
    c_core = send(C_CORE, cb, co, core)
    for copy in own_x:
        copy.wait()
    x_core = {}
    for d in (2, 1, 3, 0):
        x_core[d] = send(X_CORE + d, xb.at[2 * turn(zh, d) + 1 - c], xo.at[d], core)

    for k in range(32):
        slab_copy(k).wait()
    a0, a1 = [], []
    for d in (1, 2, 3):
        a0.append(send(RS_A0 + d - 1, slab.at[pl.ds(2 * turn(x, d), 2), :, 0:HR], ra0.at[d - 1], at_x(d)))
        a1.append(send(RS_A1 + d - 1, slab.at[:, turn(y, d), HR:ROWS], ra1.at[d - 1], at_y(d)))

    def gradient(d):
        x_core[d].wait_recv()
        dims = (((0,), (0,)), ((), ()))
        mine = lax.dot_general(xb[2 * turn(zh, d) + c], cb[...], dims, preferred_element_type=F32)
        g[d] = mine
        other = lax.dot_general(xo[d], co[...], dims, preferred_element_type=F32)
        g[d] += other

    def pack(slot, d, lo):
        def one(i, _):
            at = pl.multiple_of(i * 32, 32)
            sb[slot, pl.ds(at, 32)] = packed(g[d, pl.ds(lo + at, 32)])
            return 0
        lax.fori_loop(0, HB // 32, one, 0)

    def join(ref, half, d, lo, slot=None):
        def one(i, _):
            at = pl.multiple_of(i * 32, 32)
            total = g[d, pl.ds(lo + at, 32)] + unpacked(ref[half, pl.ds(at, 32)])
            if slot is None:
                g[d, pl.ds(lo + at, 32)] = total
            else:
                sb[slot, pl.ds(at, 32)] = packed(total)
            return 0
        lax.fori_loop(0, HB // 32, one, 0)

    c_core.wait_recv()
    gradient(2)
    pack(0, 2, 0)
    g_up1 = send(G_UP1, sb.at[0], r1.at[0], up)
    pack(1, 2, HB)
    g_down1 = send(G_DOWN1, sb.at[1], r1.at[1], down)
    gradient(1)
    pack(2, 1, HB)
    g_up = send(G_UP, sb.at[2], ru.at[0], up)
    gradient(3)
    pack(3, 3, 0)
    g_down = send(G_DOWN, sb.at[3], ru.at[1], down)
    gradient(0)

    def project(k, start=False):
        part = jnp.dot(xb[k], wb[k], preferred_element_type=F32)
        if start:
            acc[...] = part
        else:
            acc[...] += part

    project(f, True)

    for copy in a0:
        copy.wait_recv()
    for kk in range(2):
        for yy in range(4):
            pa0[kk, yy] = (
                slab[2 * x + kk, yy, 0:HR].astype(F32) + ra0[0, kk, yy].astype(F32)
                + ra0[1, kk, yy].astype(F32) + ra0[2, kk, yy].astype(F32)
            )
    b0 = [send(RS_B0 + d - 1, pa0.at[:, turn(y, d)], rb0.at[d - 1], at_y(d)) for d in (1, 2, 3)]
    for copy in a1:
        copy.wait_recv()
    for k in range(8):
        pa1[k] = (
            slab[k, y, HR:ROWS].astype(F32) + ra1[0, k].astype(F32)
            + ra1[1, k].astype(F32) + ra1[2, k].astype(F32)
        )
    b1 = [send(RS_B1 + d - 1, pa1.at[pl.ds(2 * turn(x, d), 2)], rb1.at[d - 1], at_x(d)) for d in (1, 2, 3)]
    for copy in b0:
        copy.wait_recv()
    for copy in b1:
        copy.wait_recv()
    for kk in range(2):
        tb[kk, 0:HR] = pa0[kk, y] + rb0[0, kk] + rb0[1, kk] + rb0[2, kk]
        tb[kk, HR:ROWS] = pa1[2 * x + kk] + rb1[0, kk] + rb1[1, kk] + rb1[2, kk]
    z_sum = send(RS_Z, tb.at[1 - zl], rz, pair)

    w_core.wait_recv()
    project(2 * zh + 1 - c)

    w_up.wait_recv()
    below = 2 * turn(zh, -1) + c
    w_up2 = send(W_UP2, wb.at[below, 0:HB], wb.at[below, 0:HB], up)
    w_core_up = send(W_CORE_UP, wb.at[below], wb.at[below], core)
    w_down.wait_recv()
    above = 2 * turn(zh, 1) + c
    w_down2 = send(W_DOWN2, wb.at[above, HB:B], wb.at[above, HB:B], down)
    w_core_down = send(W_CORE_DOWN, wb.at[above], wb.at[above], core)

    z_sum.wait_recv()
    own_po.wait()
    own_pm.wait()
    average = (tb[zl] + rz[...]) / REPLICAS
    pseudo_grad = po[...] - average
    new_momentum = OUTER_MOMENTUM * pm[...] + pseudo_grad
    new_outer = po[...] - OUTER_RATE * (pseudo_grad + OUTER_MOMENTUM * new_momentum)
    mom_out[...] = new_momentum
    outer_out[...] = new_outer
    agb[2 * x + zl, y] = new_outer
    z_gather = send(AG_Z, agb.at[2 * x + zl, y], agb.at[2 * x + zl, y], pair)

    g_up1.wait_recv()
    join(r1, 0, 1, 0, 4)
    g_up2 = send(G_UP2, sb.at[4], ra.at[0], up)
    g_down1.wait_recv()
    join(r1, 1, 3, HB, 5)
    g_down2 = send(G_DOWN2, sb.at[5], ra.at[1], down)

    z_gather.wait_recv()
    g0 = [send(AG_A0 + d - 1, agb.at[pl.ds(2 * x, 2), y, 0:HR], agb.at[pl.ds(2 * x, 2), y, 0:HR], at_x(d)) for d in (1, 2, 3)]
    g1 = [send(AG_A1 + d - 1, agb.at[pl.ds(2 * x, 2), y, HR:ROWS], agb.at[pl.ds(2 * x, 2), y, HR:ROWS], at_y(d)) for d in (1, 2, 3)]
    w_core_up.wait_recv()
    w_core_down.wait_recv()
    for s in (-1, 1):
        project(2 * turn(zh, s) + c)
        project(2 * turn(zh, s) + 1 - c)
    for copy in g0:
        copy.wait_recv()
    h0 = [send(AG_B0 + d - 1, agb.at[:, y, 0:HR], agb.at[:, y, 0:HR], at_y(d)) for d in (1, 2, 3)]
    for copy in g1:
        copy.wait_recv()
    h1 = [send(AG_B1 + d - 1, agb.at[pl.ds(2 * x, 2), :, HR:ROWS], agb.at[pl.ds(2 * x, 2), :, HR:ROWS], at_x(d)) for d in (1, 2, 3)]

    g_up.wait_recv()
    join(ru, 0, 0, HB)
    g_down.wait_recv()
    join(ru, 1, 0, 0)

    for copy in h0:
        copy.wait_recv()
    for copy in h1:
        copy.wait_recv()
    for k in range(32):
        block = MERGE_WEIGHT * slab[k // 4, k % 4].astype(F32) + (1.0 - MERGE_WEIGHT) * agb[k // 4, k % 4]
        local_out[:, k * LANES:(k + 1) * LANES] = block.astype(BF16)

    far = 2 * turn(zh, 2) + c
    w_up2.wait_recv()
    w_far = send(W_CORE_FAR, wb.at[far, 0:HB], wb.at[far, 0:HB], core)
    w_down2.wait_recv()
    w_far2 = send(W_CORE_FAR2, wb.at[far, HB:B], wb.at[far, HB:B], core)
    project(far)
    w_far.wait_recv()
    w_far2.wait_recv()
    project(2 * turn(zh, 2) + 1 - c)
    proj_out[...] = acc[...].astype(BF16)

    own_m1.wait()
    own_m2.wait()

    def adam(part, half):
        def body(at):
            grad = g[0, at] + unpacked(ra[half, pl.ds(at.start - half * HB, at.size)])
            new_first = BETA_ONE * m1[at] + (1.0 - BETA_ONE) * grad
            new_second = BETA_TWO * m2[at] + (1.0 - BETA_TWO) * grad * grad
            weight = wb[f, at].astype(F32)
            update = new_first / FIRST_FIX / (jnp.sqrt(new_second / SECOND_FIX) + EPSILON) + DECAY_RATE * weight
            first_out[at] = new_first
            second_out[at] = new_second
            neww_out[at] = (weight - INNER_RATE * update).astype(BF16)

        def one(i, _):
            body(pl.ds(pl.multiple_of(half * HB + i * 32, 32), 32))
            return 0
        lax.fori_loop(0, HB // 32, one, 0)

    g_up2.wait_recv()
    adam(g_up2, 0)
    g_down2.wait_recv()
    adam(g_down2, 1)
    for copy in sent:
        copy.wait_send()


def shards(tokens, key_cotangent, key_weight, first_moment, second_moment, local_slab, outer_params, outer_momentum):
    out_shape = (
        jax.ShapeDtypeStruct((B, B), BF16),
        jax.ShapeDtypeStruct((B, B), BF16),
        jax.ShapeDtypeStruct((B, B), F32),
        jax.ShapeDtypeStruct((B, B), F32),
        jax.ShapeDtypeStruct((ROWS, LANES), F32),
        jax.ShapeDtypeStruct((ROWS, LANES), F32),
        jax.ShapeDtypeStruct((ROWS, 4096), BF16),
    )
    vmem = pltpu.VMEM
    results = pl.pallas_call(
        kernel,
        out_shape=tuple(pltpu.VMEM(o.shape, o.dtype) for o in out_shape),
        in_specs=[pl.BlockSpec(memory_space=pl.ANY)] * 8,
        out_specs=(pl.BlockSpec(memory_space=pltpu.VMEM),) * 7,
        scratch_shapes=[
            vmem((8, B, B), BF16),
            vmem((4, B, B), BF16),
            vmem((B, B), BF16),
            vmem((B, B), BF16),
            vmem((8, B, B), BF16),
            vmem((4, B, B), F32),
            vmem((6, HB, B), BF16),
            vmem((2, HB, B), BF16),
            vmem((2, HB, B), BF16),
            vmem((2, HB, B), BF16),
            vmem((B, B), F32),
            vmem((B, B), F32),
            vmem((8, 4, ROWS, LANES), BF16),
            vmem((3, 2, 4, HR, LANES), BF16),
            vmem((3, 8, HR, LANES), BF16),
            vmem((2, 4, HR, LANES), F32),
            vmem((8, HR, LANES), F32),
            vmem((3, 2, HR, LANES), F32),
            vmem((3, 2, HR, LANES), F32),
            vmem((2, ROWS, LANES), F32),
            vmem((ROWS, LANES), F32),
            vmem((ROWS, LANES), F32),
            vmem((ROWS, LANES), F32),
            vmem((8, 4, ROWS, LANES), F32),
            vmem((B, B), F32),
            pltpu.SemaphoreType.DMA((N_REMOTE,)),
            pltpu.SemaphoreType.DMA((N_REMOTE,)),
            pltpu.SemaphoreType.DMA((6,)),
            pltpu.SemaphoreType.DMA((8,)),
            pltpu.SemaphoreType.DMA((32,)),
        ],
        name="window",
        compiler_params=pltpu.CompilerParams(
            collective_id=0, has_side_effects=True, vmem_limit_bytes=40 << 20
        ),
    )(*[pltpu.with_memory_space_constraint(a, pltpu.HBM) for a in (tokens, key_cotangent, key_weight, first_moment, second_moment, local_slab, outer_params, outer_momentum)])

    def deliver(*refs):
        copies = [pltpu.make_async_copy(refs[i], refs[7 + i], refs[14].at[i]) for i in range(7)]
        for copy in copies:
            copy.start()
        for copy in copies:
            copy.wait()

    return pl.pallas_call(
        deliver,
        out_shape=out_shape,
        in_specs=[pl.BlockSpec(memory_space=pltpu.VMEM)] * 7,
        out_specs=(pl.BlockSpec(memory_space=pl.ANY),) * 7,
        scratch_shapes=[pltpu.SemaphoreType.DMA((7,))],
        name="deliver",
        compiler_params=pltpu.CompilerParams(vmem_limit_bytes=8 << 20),
    )(*results)


def solution(mesh):
    both = P(("replica", "fsdp"), None)
    cut = P("fsdp", "replica")
    return jax.shard_map(
        shards,
        mesh=mesh,
        in_specs=(both, both, both, both, both, both, cut, cut),
        out_specs=(both, both, both, both, cut, cut, both),
        check_vma=False,
    )
```

```python
import jax
import jax.numpy as jnp
from jax import lax
from jax.experimental import pallas as pl
from jax.experimental.pallas import tpu as pltpu
from jax.sharding import PartitionSpec as P

BETA_ONE = 0.9
BETA_TWO = 0.95
INNER_RATE = 0.001
DECAY_RATE = 0.1
EPSILON = 1e-08
FIRST_FIX = 1.0 - (0.9**50) ** 2
SECOND_FIX = 1.0 - (0.95**50) ** 2
OUTER_RATE = 0.7
OUTER_MOMENTUM = 0.9
MERGE_WEIGHT = 0.5

MESH = pl.DeviceIdType.MESH
F32, BF16 = jnp.float32, jnp.bfloat16
B = 512
HB = 256
ROWS = 192
HR = 96
LANES = 128
REPLICAS = 32

NZ = 1

W_CORE, W_UP2, W_DOWN2, W_CORE_UP, W_CORE_DOWN, W_CORE_FAR, W_CORE_FAR2 = range(7)
C_CORE = 9
X_CORE = 10
G_UP1, G_DOWN1, G_UP, G_DOWN, G_UP2, G_DOWN2 = range(14, 20)
S_FIRST = 20
RS_A0, RS_A1, RS_B0, RS_B1 = 26, 29, 32, 35
AG_A0, AG_A1, AG_B0, AG_B1 = 38, 41, 44, 47
RS_Z = 50
AG_Z = RS_Z + NZ
W_UP = AG_Z + NZ
W_DOWN = W_UP + 4
N_REMOTE = W_DOWN + 4


TOP = 2.0**7.75


def packed(t):
    t2 = t * t
    t4 = t2 * t2
    t8 = t4 * t4
    t16 = t8 * t8
    return jnp.where(t < 0.0, -t16, t16).astype(BF16)


def unpacked(p):
    p = p.astype(F32)
    t = jnp.sqrt(jnp.sqrt(jnp.sqrt(jnp.sqrt(jnp.abs(p)))))
    return jnp.where(p < 0.0, -t, t)


def kernel(
    tok_ref, cot_ref, w_ref, first_ref, second_ref, slab_ref, outer_ref, mom_ref,
    proj_out, neww_out, first_out, second_out, outer_out, mom_out, local_out,
    xb, xo, cb, co, wb, g, sb, sc, tiles, rg, rc, m1, m2,
    slab, ra0, ra1, pa0, pa1, rb0, rb1, tb, rz, po, pm, agb, acc,
    ss, rs, ls, xs, slab_s,
):
    r = lax.axis_index("replica")
    f = lax.axis_index("fsdp")
    x, zl, y = lax.div(r, 8), lax.rem(lax.div(r, 4), 2), lax.rem(r, 4)
    zh, c = lax.div(f, 2), lax.rem(f, 2)

    def turn(value, step, size=4):
        return lax.rem(value + step + size, size)

    def dev(x_, zl_, y_, zh_, c_):
        return {"replica": (x_ * 2 + zl_) * 4 + y_, "fsdp": zh_ * 2 + c_}

    def at_x(d):
        return dev(turn(x, d), zl, y, zh, c)

    def at_y(d):
        return dev(x, zl, turn(y, d), zh, c)

    up, down = dev(x, zl, y, turn(zh, 1), c), dev(x, zl, y, turn(zh, -1), c)
    pair = dev(x, 1 - zl, y, zh, c)
    core = dev(x, zl, y, zh, 1 - c)

    def remote(place, src, dst, device):
        return pltpu.make_async_remote_copy(
            src_ref=src, dst_ref=dst, send_sem=ss.at[place], recv_sem=rs.at[place],
            device_id=device, device_id_type=MESH,
        )

    sent = []

    def send(place, src, dst, device):
        copy = remote(place, src, dst, device)
        copy.start()
        sent.append(copy)
        return copy

    own_w = pltpu.make_async_copy(w_ref, wb.at[f], ls.at[0])
    own_w.start()
    own_c = pltpu.make_async_copy(cot_ref, cb, ls.at[1])
    own_c.start()
    own_x = []
    for k in range(8):
        copy = pltpu.make_async_copy(tok_ref.at[:, k * B:(k + 1) * B], xb.at[k], xs.at[k])
        copy.start()
        own_x.append(copy)

    def slab_copy(k):
        return pltpu.make_async_copy(
            slab_ref.at[:, k * LANES:(k + 1) * LANES], slab.at[k // 4, k % 4], slab_s.at[k]
        )
    for k in range(32):
        slab_copy(k).start()
    own_m1 = pltpu.make_async_copy(first_ref, m1, ls.at[2])
    own_m2 = pltpu.make_async_copy(second_ref, m2, ls.at[3])
    own_po = pltpu.make_async_copy(outer_ref, po, ls.at[4])
    own_pm = pltpu.make_async_copy(mom_ref, pm, ls.at[5])
    for copy in (own_po, own_pm, own_m1, own_m2):
        copy.start()

    barrier = pltpu.get_barrier_semaphore()
    partners = [up, down, core, pair] + [at_x(d) for d in (1, 2, 3)] + [at_y(d) for d in (1, 2, 3)]
    for partner in partners:
        pl.semaphore_signal(barrier, inc=1, device_id=partner, device_id_type=MESH)
    pl.semaphore_wait(barrier, len(partners))

    copies = {}

    def arrived(*names):
        for name in names:
            copies[name].wait_recv()

    def send_w(*parts):
        for i in parts:
            for name, place, device, at in (("w_up", W_UP, up, i), ("w_down", W_DOWN, down, 3 - i)):
                part = wb.at[f, at * 128:(at + 1) * 128]
                copies[name, i] = send(place + i, part, part, device)

    def send_core():
        own_c.wait()
        copies["c_core"] = send(C_CORE, cb, co, core)
        for copy in own_x:
            copy.wait()
        for d in (2, 1, 3, 0):
            copies["x_core", d] = send(X_CORE + d, xb.at[2 * turn(zh, d) + 1 - c], xo.at[d], core)

    def send_w_core():
        copies["w_core"] = send(W_CORE, wb.at[f], wb.at[f], core)

    def frag_send():
        for k in range(32):
            slab_copy(k).wait()
        for d in (1, 2, 3):
            copies["a0", d] = send(RS_A0 + d - 1, slab.at[pl.ds(2 * turn(x, d), 2), :, 0:HR], ra0.at[d - 1], at_x(d))
            copies["a1", d] = send(RS_A1 + d - 1, slab.at[:, turn(y, d), HR:ROWS], ra1.at[d - 1], at_y(d))

    def gradient(d):
        arrived(("x_core", d))
        dims = (((0,), (0,)), ((), ()))
        g[d] = lax.dot_general(xb[2 * turn(zh, d) + c], cb[...], dims, preferred_element_type=F32)
        g[d] += lax.dot_general(xo[d], co[...], dims, preferred_element_type=F32)

    def chunks(body):
        def one(i, _):
            body(pl.multiple_of(i * 32, 32))
            return 0
        lax.fori_loop(0, HB // 32, one, 0)

    def spread(tile):
        wide = jnp.concatenate([tile] * 4, axis=1)
        return jnp.concatenate([wide] * 4, axis=0)

    def scale_tile(slot, d, lo):
        tiles[0] = jnp.zeros((32, B), F32)

        def body(at):
            tiles[0] = jnp.maximum(tiles[0], jnp.abs(g[d, pl.ds(lo + at, 32)]))
        chunks(body)
        top = tiles[0]
        top = jnp.maximum(jnp.maximum(top[0:8], top[8:16]), jnp.maximum(top[16:24], top[24:32]))
        top = jnp.maximum(jnp.maximum(top[:, 0:128], top[:, 128:256]), jnp.maximum(top[:, 256:384], top[:, 384:512]))
        top = jnp.maximum(top, 1e-30)
        sc[slot] = top
        tiles[0] = spread(TOP / top)

    def pack(slot, d, lo):
        scale_tile(slot, d, lo)

        def body(at):
            sb[slot, pl.ds(at, 32)] = packed(g[d, pl.ds(lo + at, 32)] * tiles[0])
        chunks(body)

    def join(half, d, lo):
        tiles[1] = spread(rc[half] * (1.0 / TOP))

        def body(at):
            g[d, pl.ds(lo + at, 32)] += unpacked(rg[half, pl.ds(at, 32)]) * tiles[1]
        chunks(body)

    def send_g(name, place, slot, device):
        copies[name] = send(place, sb.at[slot], rg.at[slot], device)
        copies[name + "s"] = send(S_FIRST + slot, sc.at[slot], rc.at[slot], device)

    def arrived_g(*names):
        for name in names:
            arrived(name, name + "s")

    def grad_first():
        arrived("c_core")
        gradient(2)
        pack(0, 2, 0)
        send_g("g_up1", G_UP1, 0, up)
        pack(1, 2, HB)
        send_g("g_down1", G_DOWN1, 1, down)

    def grad_near():
        gradient(1)
        pack(2, 1, HB)
        gradient(3)
        pack(3, 3, 0)

    def send_near():
        send_g("g_up", G_UP, 2, up)
        send_g("g_down", G_DOWN, 3, down)

    def grad_join():
        arrived_g("g_up1")
        join(0, 1, 0)
        pack(4, 1, 0)
        send_g("g_up2", G_UP2, 4, up)
        arrived_g("g_down1")
        join(1, 3, HB)
        pack(5, 3, HB)
        send_g("g_down2", G_DOWN2, 5, down)

    def grad_fold():
        arrived_g("g_up")
        join(2, 0, HB)
        arrived_g("g_down")
        join(3, 0, 0)

    def project(k, start=False):
        part = jnp.dot(xb[k], wb[k], preferred_element_type=F32)
        if start:
            acc[...] = part
        else:
            acc[...] += part

    def project_core():
        arrived("w_core")
        project(2 * zh + 1 - c)

    def frag_a():
        arrived(("a0", 1), ("a0", 2), ("a0", 3))
        for kk in range(2):
            for yy in range(4):
                pa0[kk, yy] = (
                    slab[2 * x + kk, yy, 0:HR].astype(F32) + ra0[0, kk, yy].astype(F32)
                    + ra0[1, kk, yy].astype(F32) + ra0[2, kk, yy].astype(F32)
                )
        for d in (1, 2, 3):
            copies["b0", d] = send(RS_B0 + d - 1, pa0.at[:, turn(y, d)], rb0.at[d - 1], at_y(d))
        arrived(("a1", 1), ("a1", 2), ("a1", 3))
        for k in range(8):
            pa1[k] = (
                slab[k, y, HR:ROWS].astype(F32) + ra1[0, k].astype(F32)
                + ra1[1, k].astype(F32) + ra1[2, k].astype(F32)
            )
        for d in (1, 2, 3):
            copies["b1", d] = send(RS_B1 + d - 1, pa1.at[pl.ds(2 * turn(x, d), 2)], rb1.at[d - 1], at_x(d))

    def frag_b():
        for d in (1, 2, 3):
            arrived(("b0", d), ("b1", d))
        for kk in range(2):
            tb[kk, 0:HR] = pa0[kk, y] + rb0[0, kk] + rb0[1, kk] + rb0[2, kk]
            tb[kk, HR:ROWS] = pa1[2 * x + kk] + rb1[0, kk] + rb1[1, kk] + rb1[2, kk]
        for i in range(NZ):
            part = pl.ds(i * (ROWS // NZ), ROWS // NZ)
            copies["z_sum", i] = send(RS_Z + i, tb.at[1 - zl, part], rz.at[part], pair)

    below, above, far = 2 * turn(zh, -1) + c, 2 * turn(zh, 1) + c, 2 * turn(zh, 2) + c

    def w_on():
        arrived(("w_up", 0), ("w_up", 1))
        copies["w_up2"] = send(W_UP2, wb.at[below, 0:HB], wb.at[below, 0:HB], up)
        arrived(("w_down", 0), ("w_down", 1))
        copies["w_down2"] = send(W_DOWN2, wb.at[above, HB:B], wb.at[above, HB:B], down)

    def w_share():
        arrived(("w_up", 2), ("w_up", 3))
        copies["w_core_up"] = send(W_CORE_UP, wb.at[below], wb.at[below], core)
        arrived(("w_down", 2), ("w_down", 3))
        copies["w_core_down"] = send(W_CORE_DOWN, wb.at[above], wb.at[above], core)

    def frag_update():
        arrived(*[("z_sum", i) for i in range(NZ)])
        own_po.wait()
        own_pm.wait()
        average = (tb[zl] + rz[...]) / REPLICAS
        pseudo_grad = po[...] - average
        new_momentum = OUTER_MOMENTUM * pm[...] + pseudo_grad
        new_outer = po[...] - OUTER_RATE * (pseudo_grad + OUTER_MOMENTUM * new_momentum)
        mom_out[...] = new_momentum
        outer_out[...] = new_outer
        agb[2 * x + zl, y] = new_outer
        for i in range(NZ):
            part = agb.at[2 * x + zl, y, pl.ds(i * (ROWS // NZ), ROWS // NZ)]
            copies["z_gather", i] = send(AG_Z + i, part, part, pair)

    def frag_c():
        arrived(*[("z_gather", i) for i in range(NZ)])
        for d in (1, 2, 3):
            lower, upper = agb.at[pl.ds(2 * x, 2), y, 0:HR], agb.at[pl.ds(2 * x, 2), y, HR:ROWS]
            copies["c0", d] = send(AG_A0 + d - 1, lower, lower, at_x(d))
            copies["c1", d] = send(AG_A1 + d - 1, upper, upper, at_y(d))

    def frag_d():
        arrived(("c0", 1), ("c0", 2), ("c0", 3))
        for d in (1, 2, 3):
            lower = agb.at[:, y, 0:HR]
            copies["d0", d] = send(AG_B0 + d - 1, lower, lower, at_y(d))
        arrived(("c1", 1), ("c1", 2), ("c1", 3))
        for d in (1, 2, 3):
            upper = agb.at[pl.ds(2 * x, 2), :, HR:ROWS]
            copies["d1", d] = send(AG_B1 + d - 1, upper, upper, at_x(d))

    def frag_merge():
        for d in (1, 2, 3):
            arrived(("d0", d), ("d1", d))
        for k in range(32):
            block = MERGE_WEIGHT * slab[k // 4, k % 4].astype(F32) + (1.0 - MERGE_WEIGHT) * agb[k // 4, k % 4]
            local_out[:, k * LANES:(k + 1) * LANES] = block.astype(BF16)

    def project_near():
        arrived("w_core_up", "w_core_down")
        for s in (-1, 1):
            project(2 * turn(zh, s) + c)
            project(2 * turn(zh, s) + 1 - c)

    def w_far():
        arrived("w_up2")
        copies["w_far"] = send(W_CORE_FAR, wb.at[far, 0:HB], wb.at[far, 0:HB], core)
        arrived("w_down2")
        copies["w_far2"] = send(W_CORE_FAR2, wb.at[far, HB:B], wb.at[far, HB:B], core)

    def project_far():
        project(far)
        arrived("w_far", "w_far2")
        project(2 * turn(zh, 2) + 1 - c)
        proj_out[...] = acc[...].astype(BF16)

    def adam(half):
        tiles[1] = spread(rc[4 + half] * (1.0 / TOP))

        def body(at):
            rows_at = pl.ds(half * HB + at, 32)
            grad = g[0, rows_at] + unpacked(rg[4 + half, pl.ds(at, 32)]) * tiles[1]
            new_first = BETA_ONE * m1[rows_at] + (1.0 - BETA_ONE) * grad
            new_second = BETA_TWO * m2[rows_at] + (1.0 - BETA_TWO) * grad * grad
            weight = wb[f, rows_at].astype(F32)
            update = new_first / FIRST_FIX / (jnp.sqrt(new_second / SECOND_FIX) + EPSILON) + DECAY_RATE * weight
            first_out[rows_at] = new_first
            second_out[rows_at] = new_second
            neww_out[rows_at] = (weight - INNER_RATE * update).astype(BF16)
        chunks(body)

    def inner():
        own_m1.wait()
        own_m2.wait()
        arrived_g("g_up2")
        adam(0)
        arrived_g("g_down2")
        adam(1)

    own_w.wait()
    send_w(0, 1)
    send_core()
    send_w_core()
    frag_send()
    grad_first()
    grad_near()
    gradient(0)
    project(f, True)
    frag_a()
    project_core()
    frag_b()
    send_w(2)
    frag_update()
    send_w(3)
    grad_join()
    frag_c()
    send_near()
    w_on()
    w_share()
    project_near()
    frag_d()
    grad_fold()
    frag_merge()
    inner()
    w_far()
    project_far()
    for copy in sent:
        copy.wait_send()


def shards(tokens, key_cotangent, key_weight, first_moment, second_moment, local_slab, outer_params, outer_momentum):
    out_shape = (
        jax.ShapeDtypeStruct((B, B), BF16),
        jax.ShapeDtypeStruct((B, B), BF16),
        jax.ShapeDtypeStruct((B, B), F32),
        jax.ShapeDtypeStruct((B, B), F32),
        jax.ShapeDtypeStruct((ROWS, LANES), F32),
        jax.ShapeDtypeStruct((ROWS, LANES), F32),
        jax.ShapeDtypeStruct((ROWS, 4096), BF16),
    )
    vmem = pltpu.VMEM
    results = pl.pallas_call(
        kernel,
        out_shape=tuple(pltpu.VMEM(o.shape, o.dtype) for o in out_shape),
        in_specs=[pl.BlockSpec(memory_space=pl.ANY)] * 8,
        out_specs=(pl.BlockSpec(memory_space=pltpu.VMEM),) * 7,
        scratch_shapes=[
            vmem((8, B, B), BF16),
            vmem((4, B, B), BF16),
            vmem((B, B), BF16),
            vmem((B, B), BF16),
            vmem((8, B, B), BF16),
            vmem((4, B, B), F32),
            vmem((6, HB, B), BF16),
            vmem((6, 8, LANES), F32),
            vmem((2, 32, B), F32),
            vmem((6, HB, B), BF16),
            vmem((6, 8, LANES), F32),
            vmem((B, B), F32),
            vmem((B, B), F32),
            vmem((8, 4, ROWS, LANES), BF16),
            vmem((3, 2, 4, HR, LANES), BF16),
            vmem((3, 8, HR, LANES), BF16),
            vmem((2, 4, HR, LANES), F32),
            vmem((8, HR, LANES), F32),
            vmem((3, 2, HR, LANES), F32),
            vmem((3, 2, HR, LANES), F32),
            vmem((2, ROWS, LANES), F32),
            vmem((ROWS, LANES), F32),
            vmem((ROWS, LANES), F32),
            vmem((ROWS, LANES), F32),
            vmem((8, 4, ROWS, LANES), F32),
            vmem((B, B), F32),
            pltpu.SemaphoreType.DMA((N_REMOTE,)),
            pltpu.SemaphoreType.DMA((N_REMOTE,)),
            pltpu.SemaphoreType.DMA((6,)),
            pltpu.SemaphoreType.DMA((8,)),
            pltpu.SemaphoreType.DMA((32,)),
        ],
        name="window",
        compiler_params=pltpu.CompilerParams(
            collective_id=0, has_side_effects=True, vmem_limit_bytes=40 << 20
        ),
    )(*[pltpu.with_memory_space_constraint(a, pltpu.HBM) for a in (tokens, key_cotangent, key_weight, first_moment, second_moment, local_slab, outer_params, outer_momentum)])

    def deliver(*refs):
        copies = [pltpu.make_async_copy(refs[i], refs[7 + i], refs[14].at[i]) for i in range(7)]
        for copy in copies:
            copy.start()
        for copy in copies:
            copy.wait()

    return pl.pallas_call(
        deliver,
        out_shape=out_shape,
        in_specs=[pl.BlockSpec(memory_space=pltpu.VMEM)] * 7,
        out_specs=(pl.BlockSpec(memory_space=pl.ANY),) * 7,
        scratch_shapes=[pltpu.SemaphoreType.DMA((7,))],
        name="deliver",
        compiler_params=pltpu.CompilerParams(vmem_limit_bytes=8 << 20),
    )(*results)


def solution(mesh):
    both = P(("replica", "fsdp"), None)
    cut = P("fsdp", "replica")
    return jax.shard_map(
        shards,
        mesh=mesh,
        in_specs=(both, both, both, both, both, both, cut, cut),
        out_specs=(both, both, both, both, cut, cut, both),
        check_vma=False,
    )
```

```python
import jax
import jax.numpy as jnp
from jax import lax
from jax.experimental import pallas as pl
from jax.experimental.pallas import tpu as pltpu
from jax.sharding import PartitionSpec as P

BETA_ONE = 0.9
BETA_TWO = 0.95
INNER_RATE = 0.001
DECAY_RATE = 0.1
EPSILON = 1e-08
FIRST_FIX = 1.0 - (0.9**50) ** 2
SECOND_FIX = 1.0 - (0.95**50) ** 2
OUTER_RATE = 0.7
OUTER_MOMENTUM = 0.9
MERGE_WEIGHT = 0.5

MESH = pl.DeviceIdType.MESH
F32, BF16 = jnp.float32, jnp.bfloat16
B = 512
HB = 256
ROWS = 192
HR = 96
LANES = 128
REPLICAS = 32

NZ = 1

W_CORE, W_UP2, W_DOWN2, W_CORE_UP, W_CORE_DOWN, W_CORE_FAR, W_CORE_FAR2 = range(7)
C_CORE = 9
X_CORE = 10
G_UP1, G_DOWN1, G_UP, G_DOWN, G_UP2, G_DOWN2 = range(14, 20)
S_FIRST = 20
RS_A0, RS_A1, RS_B0, RS_B1 = 26, 29, 32, 35
AG_A0, AG_A1, AG_B0, AG_B1 = 38, 41, 44, 47
RS_Z = 50
AG_Z = RS_Z + NZ
W_UP = AG_Z + NZ
W_DOWN = W_UP + 4
N_REMOTE = W_DOWN + 4


TOP = 2.0**7.75


def packed(t):
    t2 = t * t
    t4 = t2 * t2
    t8 = t4 * t4
    t16 = t8 * t8
    return jnp.where(t < 0.0, -t16, t16).astype(BF16)


def unpacked(p):
    p = p.astype(F32)
    t = jnp.sqrt(jnp.sqrt(jnp.sqrt(jnp.sqrt(jnp.abs(p)))))
    return jnp.where(p < 0.0, -t, t)


def kernel(
    tok_ref, cot_ref, w_ref, first_ref, second_ref, slab_ref, outer_ref, mom_ref,
    proj_out, neww_out, first_out, second_out, outer_out, mom_out, local_out,
    xb, xo, cb, co, wb, g, sb, sc, tiles, rg, rc, m1, m2,
    slab, ra0, ra1, pa0, pa1, rb0, rb1, tb, rz, po, pm, agb, acc,
    ss, rs, ls, xs, slab_s,
):
    r = lax.axis_index("replica")
    f = lax.axis_index("fsdp")
    x, zl, y = lax.div(r, 8), lax.rem(lax.div(r, 4), 2), lax.rem(r, 4)
    zh, c = lax.div(f, 2), lax.rem(f, 2)

    def turn(value, step, size=4):
        return lax.rem(value + step + size, size)

    def dev(x_, zl_, y_, zh_, c_):
        return {"replica": (x_ * 2 + zl_) * 4 + y_, "fsdp": zh_ * 2 + c_}

    def at_x(d):
        return dev(turn(x, d), zl, y, zh, c)

    def at_y(d):
        return dev(x, zl, turn(y, d), zh, c)

    up, down = dev(x, zl, y, turn(zh, 1), c), dev(x, zl, y, turn(zh, -1), c)
    pair = dev(x, 1 - zl, y, zh, c)
    core = dev(x, zl, y, zh, 1 - c)

    def remote(place, src, dst, device):
        return pltpu.make_async_remote_copy(
            src_ref=src, dst_ref=dst, send_sem=ss.at[place], recv_sem=rs.at[place],
            device_id=device, device_id_type=MESH,
        )

    sent = []

    def send(place, src, dst, device):
        copy = remote(place, src, dst, device)
        copy.start()
        sent.append(copy)
        return copy

    barrier = pltpu.get_barrier_semaphore()
    partners = [up, down, core, pair] + [at_x(d) for d in (1, 2, 3)] + [at_y(d) for d in (1, 2, 3)]
    for partner in partners:
        pl.semaphore_signal(barrier, inc=1, device_id=partner, device_id_type=MESH)

    own_w = pltpu.make_async_copy(w_ref, wb.at[f], ls.at[0])
    own_w.start()
    own_c = pltpu.make_async_copy(cot_ref, cb, ls.at[1])
    own_c.start()
    own_x = []
    for k in range(8):
        copy = pltpu.make_async_copy(tok_ref.at[:, k * B:(k + 1) * B], xb.at[k], xs.at[k])
        copy.start()
        own_x.append(copy)

    def slab_copy(k):
        return pltpu.make_async_copy(
            slab_ref.at[:, k * LANES:(k + 1) * LANES], slab.at[k // 4, k % 4], slab_s.at[k]
        )
    own_m1 = pltpu.make_async_copy(first_ref, m1, ls.at[2])
    own_m2 = pltpu.make_async_copy(second_ref, m2, ls.at[3])
    own_po = pltpu.make_async_copy(outer_ref, po, ls.at[4])
    own_pm = pltpu.make_async_copy(mom_ref, pm, ls.at[5])
    for copy in (own_po, own_pm, own_m1, own_m2):
        copy.start()

    pl.semaphore_wait(barrier, len(partners))

    copies = {}

    def arrived(*names):
        for name in names:
            copies[name].wait_recv()

    def send_w(*parts):
        for i in parts:
            for name, place, device, at in (("w_up", W_UP, up, i), ("w_down", W_DOWN, down, 3 - i)):
                part = wb.at[f, at * 128:(at + 1) * 128]
                copies[name, i] = send(place + i, part, part, device)

    def load_slab():
        for k in range(32):
            slab_copy(k).start()

    def send_core():
        own_c.wait()
        copies["c_core"] = send(C_CORE, cb, co, core)
        for copy in own_x:
            copy.wait()
        for d in (2, 1, 3, 0):
            copies["x_core", d] = send(X_CORE + d, xb.at[2 * turn(zh, d) + 1 - c], xo.at[d], core)

    def send_w_core():
        copies["w_core"] = send(W_CORE, wb.at[f], wb.at[f], core)

    def frag_send():
        for k in range(32):
            slab_copy(k).wait()
        for d in (1, 2, 3):
            copies["a0", d] = send(RS_A0 + d - 1, slab.at[pl.ds(2 * turn(x, d), 2), :, 0:HR], ra0.at[d - 1], at_x(d))
            copies["a1", d] = send(RS_A1 + d - 1, slab.at[:, turn(y, d), HR:ROWS], ra1.at[d - 1], at_y(d))

    def gradient(d):
        arrived(("x_core", d))
        dims = (((0,), (0,)), ((), ()))
        g[d] = lax.dot_general(xb[2 * turn(zh, d) + c], cb[...], dims, preferred_element_type=F32)
        g[d] += lax.dot_general(xo[d], co[...], dims, preferred_element_type=F32)

    def chunks(body):
        def one(i, _):
            body(pl.multiple_of(i * 32, 32))
            return 0
        lax.fori_loop(0, HB // 32, one, 0)

    def spread(tile):
        wide = jnp.concatenate([tile] * 4, axis=1)
        return jnp.concatenate([wide] * 4, axis=0)

    def scale_tile(slot, d, lo):
        tiles[0] = jnp.zeros((32, B), F32)

        def body(at):
            tiles[0] = jnp.maximum(tiles[0], jnp.abs(g[d, pl.ds(lo + at, 32)]))
        chunks(body)
        top = tiles[0]
        top = jnp.maximum(jnp.maximum(top[0:8], top[8:16]), jnp.maximum(top[16:24], top[24:32]))
        top = jnp.maximum(jnp.maximum(top[:, 0:128], top[:, 128:256]), jnp.maximum(top[:, 256:384], top[:, 384:512]))
        top = jnp.maximum(top, 1e-30)
        sc[slot] = top
        tiles[0] = spread(TOP / top)

    def pack(slot, d, lo):
        scale_tile(slot, d, lo)

        def body(at):
            sb[slot, pl.ds(at, 32)] = packed(g[d, pl.ds(lo + at, 32)] * tiles[0])
        chunks(body)

    def join(half, d, lo):
        tiles[1] = spread(rc[half] * (1.0 / TOP))

        def body(at):
            g[d, pl.ds(lo + at, 32)] += unpacked(rg[half, pl.ds(at, 32)]) * tiles[1]
        chunks(body)

    def send_g(name, place, slot, device):
        copies[name] = send(place, sb.at[slot], rg.at[slot], device)
        copies[name + "s"] = send(S_FIRST + slot, sc.at[slot], rc.at[slot], device)

    def arrived_g(*names):
        for name in names:
            arrived(name, name + "s")

    def grad_first():
        arrived("c_core")
        gradient(2)
        pack(0, 2, 0)
        send_g("g_up1", G_UP1, 0, up)
        pack(1, 2, HB)
        send_g("g_down1", G_DOWN1, 1, down)

    def grad_near():
        gradient(1)
        pack(2, 1, HB)
        gradient(3)
        pack(3, 3, 0)

    def send_near():
        send_g("g_up", G_UP, 2, up)
        send_g("g_down", G_DOWN, 3, down)

    def grad_join():
        arrived_g("g_up1")
        join(0, 1, 0)
        pack(4, 1, 0)
        send_g("g_up2", G_UP2, 4, up)
        arrived_g("g_down1")
        join(1, 3, HB)
        pack(5, 3, HB)
        send_g("g_down2", G_DOWN2, 5, down)

    def grad_fold():
        arrived_g("g_up")
        join(2, 0, HB)
        arrived_g("g_down")
        join(3, 0, 0)

    def project(k, start=False):
        part = jnp.dot(xb[k], wb[k], preferred_element_type=F32)
        if start:
            acc[...] = part
        else:
            acc[...] += part

    def project_core():
        arrived("w_core")
        project(2 * zh + 1 - c)

    def frag_a():
        arrived(("a0", 1), ("a0", 2), ("a0", 3))
        for kk in range(2):
            for yy in range(4):
                pa0[kk, yy] = (
                    slab[2 * x + kk, yy, 0:HR].astype(F32) + ra0[0, kk, yy].astype(F32)
                    + ra0[1, kk, yy].astype(F32) + ra0[2, kk, yy].astype(F32)
                )
        for d in (1, 2, 3):
            copies["b0", d] = send(RS_B0 + d - 1, pa0.at[:, turn(y, d)], rb0.at[d - 1], at_y(d))
        arrived(("a1", 1), ("a1", 2), ("a1", 3))
        for k in range(8):
            pa1[k] = (
                slab[k, y, HR:ROWS].astype(F32) + ra1[0, k].astype(F32)
                + ra1[1, k].astype(F32) + ra1[2, k].astype(F32)
            )
        for d in (1, 2, 3):
            copies["b1", d] = send(RS_B1 + d - 1, pa1.at[pl.ds(2 * turn(x, d), 2)], rb1.at[d - 1], at_x(d))

    def frag_b():
        for d in (1, 2, 3):
            arrived(("b0", d), ("b1", d))
        for kk in range(2):
            tb[kk, 0:HR] = pa0[kk, y] + rb0[0, kk] + rb0[1, kk] + rb0[2, kk]
            tb[kk, HR:ROWS] = pa1[2 * x + kk] + rb1[0, kk] + rb1[1, kk] + rb1[2, kk]
        for i in range(NZ):
            part = pl.ds(i * (ROWS // NZ), ROWS // NZ)
            copies["z_sum", i] = send(RS_Z + i, tb.at[1 - zl, part], rz.at[part], pair)

    below, above, far = 2 * turn(zh, -1) + c, 2 * turn(zh, 1) + c, 2 * turn(zh, 2) + c

    def w_on():
        arrived(("w_up", 0), ("w_up", 1))
        copies["w_up2"] = send(W_UP2, wb.at[below, 0:HB], wb.at[below, 0:HB], up)
        arrived(("w_down", 0), ("w_down", 1))
        copies["w_down2"] = send(W_DOWN2, wb.at[above, HB:B], wb.at[above, HB:B], down)

    def w_share():
        arrived(("w_up", 2), ("w_up", 3))
        copies["w_core_up"] = send(W_CORE_UP, wb.at[below], wb.at[below], core)
        arrived(("w_down", 2), ("w_down", 3))
        copies["w_core_down"] = send(W_CORE_DOWN, wb.at[above], wb.at[above], core)

    def frag_update():
        arrived(*[("z_sum", i) for i in range(NZ)])
        own_po.wait()
        own_pm.wait()
        average = (tb[zl] + rz[...]) / REPLICAS
        pseudo_grad = po[...] - average
        new_momentum = OUTER_MOMENTUM * pm[...] + pseudo_grad
        new_outer = po[...] - OUTER_RATE * (pseudo_grad + OUTER_MOMENTUM * new_momentum)
        mom_out[...] = new_momentum
        outer_out[...] = new_outer
        agb[2 * x + zl, y] = new_outer
        for i in range(NZ):
            part = agb.at[2 * x + zl, y, pl.ds(i * (ROWS // NZ), ROWS // NZ)]
            copies["z_gather", i] = send(AG_Z + i, part, part, pair)

    def frag_c():
        arrived(*[("z_gather", i) for i in range(NZ)])
        for d in (1, 2, 3):
            lower, upper = agb.at[pl.ds(2 * x, 2), y, 0:HR], agb.at[pl.ds(2 * x, 2), y, HR:ROWS]
            copies["c0", d] = send(AG_A0 + d - 1, lower, lower, at_x(d))
            copies["c1", d] = send(AG_A1 + d - 1, upper, upper, at_y(d))

    def frag_d():
        arrived(("c0", 1), ("c0", 2), ("c0", 3))
        for d in (1, 2, 3):
            lower = agb.at[:, y, 0:HR]
            copies["d0", d] = send(AG_B0 + d - 1, lower, lower, at_y(d))
        arrived(("c1", 1), ("c1", 2), ("c1", 3))
        for d in (1, 2, 3):
            upper = agb.at[pl.ds(2 * x, 2), :, HR:ROWS]
            copies["d1", d] = send(AG_B1 + d - 1, upper, upper, at_x(d))

    def frag_merge():
        for d in (1, 2, 3):
            arrived(("d0", d), ("d1", d))
        for k in range(32):
            block = MERGE_WEIGHT * slab[k // 4, k % 4].astype(F32) + (1.0 - MERGE_WEIGHT) * agb[k // 4, k % 4]
            local_out[:, k * LANES:(k + 1) * LANES] = block.astype(BF16)

    def project_near():
        arrived("w_core_up", "w_core_down")
        for s in (-1, 1):
            project(2 * turn(zh, s) + c)
            project(2 * turn(zh, s) + 1 - c)

    def w_far():
        arrived("w_up2")
        copies["w_far"] = send(W_CORE_FAR, wb.at[far, 0:HB], wb.at[far, 0:HB], core)
        arrived("w_down2")
        copies["w_far2"] = send(W_CORE_FAR2, wb.at[far, HB:B], wb.at[far, HB:B], core)

    def project_far():
        project(far)
        arrived("w_far", "w_far2")
        project(2 * turn(zh, 2) + 1 - c)
        proj_out[...] = acc[...].astype(BF16)

    def adam(half):
        tiles[1] = spread(rc[4 + half] * (1.0 / TOP))

        def body(at):
            rows_at = pl.ds(half * HB + at, 32)
            grad = g[0, rows_at] + unpacked(rg[4 + half, pl.ds(at, 32)]) * tiles[1]
            new_first = BETA_ONE * m1[rows_at] + (1.0 - BETA_ONE) * grad
            new_second = BETA_TWO * m2[rows_at] + (1.0 - BETA_TWO) * grad * grad
            weight = wb[f, rows_at].astype(F32)
            update = new_first / FIRST_FIX / (jnp.sqrt(new_second / SECOND_FIX) + EPSILON) + DECAY_RATE * weight
            first_out[rows_at] = new_first
            second_out[rows_at] = new_second
            neww_out[rows_at] = (weight - INNER_RATE * update).astype(BF16)
        chunks(body)

    def inner():
        own_m1.wait()
        own_m2.wait()
        arrived_g("g_up2")
        adam(0)
        arrived_g("g_down2")
        adam(1)

    own_w.wait()
    send_w(0, 1)
    load_slab()
    send_core()
    send_w_core()
    frag_send()
    grad_first()
    grad_near()
    gradient(0)
    project(f, True)
    frag_a()
    project_core()
    frag_b()
    send_w(2)
    frag_update()
    frag_c()
    send_w(3)
    grad_join()
    send_near()
    w_on()
    w_share()
    project_near()
    frag_d()
    grad_fold()
    frag_merge()
    inner()
    w_far()
    project_far()
    for copy in sent:
        copy.wait_send()


def shards(tokens, key_cotangent, key_weight, first_moment, second_moment, local_slab, outer_params, outer_momentum):
    out_shape = (
        jax.ShapeDtypeStruct((B, B), BF16),
        jax.ShapeDtypeStruct((B, B), BF16),
        jax.ShapeDtypeStruct((B, B), F32),
        jax.ShapeDtypeStruct((B, B), F32),
        jax.ShapeDtypeStruct((ROWS, LANES), F32),
        jax.ShapeDtypeStruct((ROWS, LANES), F32),
        jax.ShapeDtypeStruct((ROWS, 4096), BF16),
    )
    vmem = pltpu.VMEM
    results = pl.pallas_call(
        kernel,
        out_shape=tuple(pltpu.VMEM(o.shape, o.dtype) for o in out_shape),
        in_specs=[pl.BlockSpec(memory_space=pl.ANY)] * 8,
        out_specs=(pl.BlockSpec(memory_space=pltpu.VMEM),) * 7,
        scratch_shapes=[
            vmem((8, B, B), BF16),
            vmem((4, B, B), BF16),
            vmem((B, B), BF16),
            vmem((B, B), BF16),
            vmem((8, B, B), BF16),
            vmem((4, B, B), F32),
            vmem((6, HB, B), BF16),
            vmem((6, 8, LANES), F32),
            vmem((2, 32, B), F32),
            vmem((6, HB, B), BF16),
            vmem((6, 8, LANES), F32),
            vmem((B, B), F32),
            vmem((B, B), F32),
            vmem((8, 4, ROWS, LANES), BF16),
            vmem((3, 2, 4, HR, LANES), BF16),
            vmem((3, 8, HR, LANES), BF16),
            vmem((2, 4, HR, LANES), F32),
            vmem((8, HR, LANES), F32),
            vmem((3, 2, HR, LANES), F32),
            vmem((3, 2, HR, LANES), F32),
            vmem((2, ROWS, LANES), F32),
            vmem((ROWS, LANES), F32),
            vmem((ROWS, LANES), F32),
            vmem((ROWS, LANES), F32),
            vmem((8, 4, ROWS, LANES), F32),
            vmem((B, B), F32),
            pltpu.SemaphoreType.DMA((N_REMOTE,)),
            pltpu.SemaphoreType.DMA((N_REMOTE,)),
            pltpu.SemaphoreType.DMA((6,)),
            pltpu.SemaphoreType.DMA((8,)),
            pltpu.SemaphoreType.DMA((32,)),
        ],
        name="window",
        compiler_params=pltpu.CompilerParams(
            collective_id=0, has_side_effects=True, vmem_limit_bytes=40 << 20
        ),
    )(*[pltpu.with_memory_space_constraint(a, pltpu.HBM) for a in (tokens, key_cotangent, key_weight, first_moment, second_moment, local_slab, outer_params, outer_momentum)])

    def deliver(*refs):
        copies = [pltpu.make_async_copy(refs[i], refs[7 + i], refs[14].at[i]) for i in range(7)]
        for copy in copies:
            copy.start()
        for copy in copies:
            copy.wait()

    return pl.pallas_call(
        deliver,
        out_shape=out_shape,
        in_specs=[pl.BlockSpec(memory_space=pltpu.VMEM)] * 7,
        out_specs=(pl.BlockSpec(memory_space=pl.ANY),) * 7,
        scratch_shapes=[pltpu.SemaphoreType.DMA((7,))],
        name="deliver",
        compiler_params=pltpu.CompilerParams(vmem_limit_bytes=8 << 20),
    )(*results)


def solution(mesh):
    both = P(("replica", "fsdp"), None)
    cut = P("fsdp", "replica")
    return jax.shard_map(
        shards,
        mesh=mesh,
        in_specs=(both, both, both, both, both, both, cut, cut),
        out_specs=(both, both, both, both, cut, cut, both),
        check_vma=False,
    )
```

```python
import jax
import jax.numpy as jnp
from jax import lax
from jax.experimental import pallas as pl
from jax.experimental.pallas import tpu as pltpu
from jax.sharding import PartitionSpec as P

BETA_ONE = 0.9
BETA_TWO = 0.95
INNER_RATE = 0.001
DECAY_RATE = 0.1
EPSILON = 1e-08
FIRST_FIX = 1.0 - (0.9**50) ** 2
SECOND_FIX = 1.0 - (0.95**50) ** 2
OUTER_RATE = 0.7
OUTER_MOMENTUM = 0.9
MERGE_WEIGHT = 0.5

MESH = pl.DeviceIdType.MESH
F32, BF16 = jnp.float32, jnp.bfloat16
B = 512
HB = 256
ROWS = 192
HR = 96
LANES = 128
REPLICAS = 32

NZ = 1

W_CORE, W_UP2, W_DOWN2, W_CORE_UP, W_CORE_DOWN, W_CORE_FAR, W_CORE_FAR2 = range(7)
C_CORE = 9
X_CORE = 10
G_UP1, G_DOWN1, G_UP, G_DOWN, G_UP2, G_DOWN2 = range(14, 20)
S_FIRST = 20
RS_A0, RS_A1, RS_B0, RS_B1 = 26, 29, 32, 35
AG_A0, AG_A1, AG_B0, AG_B1 = 38, 41, 44, 47
RS_Z = 50
AG_Z = RS_Z + NZ
W_UP = AG_Z + NZ
W_DOWN = W_UP + 4
N_REMOTE = W_DOWN + 4


TOP = 2.0**7.75


def packed(t):
    t2 = t * t
    t4 = t2 * t2
    t8 = t4 * t4
    t16 = t8 * t8
    return jnp.where(t < 0.0, -t16, t16).astype(BF16)


def unpacked(p):
    p = p.astype(F32)
    t = jnp.sqrt(jnp.sqrt(jnp.sqrt(jnp.sqrt(jnp.abs(p)))))
    return jnp.where(p < 0.0, -t, t)


def kernel(
    tok_ref, cot_ref, w_ref, first_ref, second_ref, slab_ref, outer_ref, mom_ref,
    proj_out, neww_out, first_out, second_out, outer_out, mom_out, local_out,
    xb, xo, cb, co, wb, g, sb, sc, tiles, rg, rc, m1, m2,
    slab, ra0, ra1, pa0, pa1, rb0, rb1, tb, rz, po, pm, agb, acc,
    ss, rs, ls, xs, slab_s,
):
    r = lax.axis_index("replica")
    f = lax.axis_index("fsdp")
    x, zl, y = lax.div(r, 8), lax.rem(lax.div(r, 4), 2), lax.rem(r, 4)
    zh, c = lax.div(f, 2), lax.rem(f, 2)

    def turn(value, step, size=4):
        return lax.rem(value + step + size, size)

    def dev(x_, zl_, y_, zh_, c_):
        return {"replica": (x_ * 2 + zl_) * 4 + y_, "fsdp": zh_ * 2 + c_}

    def at_x(d):
        return dev(turn(x, d), zl, y, zh, c)

    def at_y(d):
        return dev(x, zl, turn(y, d), zh, c)

    up, down = dev(x, zl, y, turn(zh, 1), c), dev(x, zl, y, turn(zh, -1), c)
    pair = dev(x, 1 - zl, y, zh, c)
    core = dev(x, zl, y, zh, 1 - c)

    def remote(place, src, dst, device):
        return pltpu.make_async_remote_copy(
            src_ref=src, dst_ref=dst, send_sem=ss.at[place], recv_sem=rs.at[place],
            device_id=device, device_id_type=MESH,
        )

    sent = []

    def send(place, src, dst, device):
        copy = remote(place, src, dst, device)
        copy.start()
        sent.append(copy)
        return copy

    barrier = pltpu.get_barrier_semaphore()
    partners = [up, down, core, pair] + [at_x(d) for d in (1, 2, 3)] + [at_y(d) for d in (1, 2, 3)]
    for partner in partners:
        pl.semaphore_signal(barrier, inc=1, device_id=partner, device_id_type=MESH)

    own_w = pltpu.make_async_copy(w_ref, wb.at[f], ls.at[0])
    own_w.start()
    own_c = pltpu.make_async_copy(cot_ref, cb, ls.at[1])
    own_c.start()
    own_x = []
    for k in range(8):
        copy = pltpu.make_async_copy(tok_ref.at[:, k * B:(k + 1) * B], xb.at[k], xs.at[k])
        copy.start()
        own_x.append(copy)

    def slab_copy(k):
        return pltpu.make_async_copy(
            slab_ref.at[:, k * LANES:(k + 1) * LANES], slab.at[k // 4, k % 4], slab_s.at[k]
        )
    own_m1 = pltpu.make_async_copy(first_ref, m1, ls.at[2])
    own_m2 = pltpu.make_async_copy(second_ref, m2, ls.at[3])
    own_po = pltpu.make_async_copy(outer_ref, po, ls.at[4])
    own_pm = pltpu.make_async_copy(mom_ref, pm, ls.at[5])
    for copy in (own_po, own_pm, own_m1, own_m2):
        copy.start()

    pl.semaphore_wait(barrier, len(partners))

    copies = {}

    def arrived(*names):
        for name in names:
            copies[name].wait_recv()

    def send_w(*parts):
        for i in parts:
            for name, place, device, at in (("w_up", W_UP, up, i), ("w_down", W_DOWN, down, 3 - i)):
                part = wb.at[f, at * 128:(at + 1) * 128]
                copies[name, i] = send(place + i, part, part, device)

    def load_slab():
        for k in range(32):
            slab_copy(k).start()

    def send_core():
        own_c.wait()
        copies["c_core"] = send(C_CORE, cb, co, core)
        for copy in own_x:
            copy.wait()
        for d in (2, 1, 3, 0):
            copies["x_core", d] = send(X_CORE + d, xb.at[2 * turn(zh, d) + 1 - c], xo.at[d], core)

    def send_w_core():
        copies["w_core"] = send(W_CORE, wb.at[f], wb.at[f], core)

    def frag_send():
        for k in range(32):
            slab_copy(k).wait()
        for d in (1, 2, 3):
            copies["a0", d] = send(RS_A0 + d - 1, slab.at[pl.ds(2 * turn(x, d), 2), :, 0:HR], ra0.at[d - 1], at_x(d))
            copies["a1", d] = send(RS_A1 + d - 1, slab.at[:, turn(y, d), HR:ROWS], ra1.at[d - 1], at_y(d))

    def gradient(d):
        arrived(("x_core", d))
        dims = (((0,), (0,)), ((), ()))
        g[d] = lax.dot_general(xb[2 * turn(zh, d) + c], cb[...], dims, preferred_element_type=F32)
        g[d] += lax.dot_general(xo[d], co[...], dims, preferred_element_type=F32)

    def chunks(body):
        def one(i, _):
            body(pl.multiple_of(i * 32, 32))
            return 0
        lax.fori_loop(0, HB // 32, one, 0)

    def spread(tile):
        wide = jnp.concatenate([tile] * 4, axis=1)
        return jnp.concatenate([wide] * 4, axis=0)

    def scale_tile(slot, d, lo):
        tiles[0] = jnp.zeros((32, B), F32)

        def body(at):
            tiles[0] = jnp.maximum(tiles[0], jnp.abs(g[d, pl.ds(lo + at, 32)]))
        chunks(body)
        top = tiles[0]
        top = jnp.maximum(jnp.maximum(top[0:8], top[8:16]), jnp.maximum(top[16:24], top[24:32]))
        top = jnp.maximum(jnp.maximum(top[:, 0:128], top[:, 128:256]), jnp.maximum(top[:, 256:384], top[:, 384:512]))
        top = jnp.maximum(top, 1e-30)
        sc[slot] = top
        tiles[0] = spread(TOP / top)

    def pack(slot, d, lo):
        scale_tile(slot, d, lo)

        def body(at):
            sb[slot, pl.ds(at, 32)] = packed(g[d, pl.ds(lo + at, 32)] * tiles[0])
        chunks(body)

    def join(half, d, lo):
        tiles[1] = spread(rc[half] * (1.0 / TOP))

        def body(at):
            g[d, pl.ds(lo + at, 32)] += unpacked(rg[half, pl.ds(at, 32)]) * tiles[1]
        chunks(body)

    def send_g(name, place, slot, device):
        copies[name] = send(place, sb.at[slot], rg.at[slot], device)
        copies[name + "s"] = send(S_FIRST + slot, sc.at[slot], rc.at[slot], device)

    def arrived_g(*names):
        for name in names:
            arrived(name, name + "s")

    def grad_first():
        arrived("c_core")
        gradient(2)
        pack(0, 2, 0)
        send_g("g_up1", G_UP1, 0, up)
        pack(1, 2, HB)
        send_g("g_down1", G_DOWN1, 1, down)

    def grad_near():
        gradient(1)
        pack(2, 1, HB)
        gradient(3)
        pack(3, 3, 0)

    def send_near():
        send_g("g_up", G_UP, 2, up)
        send_g("g_down", G_DOWN, 3, down)

    def grad_join():
        arrived_g("g_up1")
        join(0, 1, 0)
        pack(4, 1, 0)
        send_g("g_up2", G_UP2, 4, up)
        arrived_g("g_down1")
        join(1, 3, HB)
        pack(5, 3, HB)
        send_g("g_down2", G_DOWN2, 5, down)

    def grad_fold():
        arrived_g("g_up")
        join(2, 0, HB)
        arrived_g("g_down")
        join(3, 0, 0)

    def project(k, start=False):
        part = jnp.dot(xb[k], wb[k], preferred_element_type=F32)
        if start:
            acc[...] = part
        else:
            acc[...] += part

    def project_core():
        arrived("w_core")
        project(2 * zh + 1 - c)

    def frag_a():
        arrived(("a0", 1), ("a0", 2), ("a0", 3))
        for kk in range(2):
            for yy in range(4):
                pa0[kk, yy] = (
                    slab[2 * x + kk, yy, 0:HR].astype(F32) + ra0[0, kk, yy].astype(F32)
                    + ra0[1, kk, yy].astype(F32) + ra0[2, kk, yy].astype(F32)
                )
        for d in (1, 2, 3):
            copies["b0", d] = send(RS_B0 + d - 1, pa0.at[:, turn(y, d)], rb0.at[d - 1], at_y(d))
        arrived(("a1", 1), ("a1", 2), ("a1", 3))
        for k in range(8):
            pa1[k] = (
                slab[k, y, HR:ROWS].astype(F32) + ra1[0, k].astype(F32)
                + ra1[1, k].astype(F32) + ra1[2, k].astype(F32)
            )
        for d in (1, 2, 3):
            copies["b1", d] = send(RS_B1 + d - 1, pa1.at[pl.ds(2 * turn(x, d), 2)], rb1.at[d - 1], at_x(d))

    def frag_b():
        for d in (1, 2, 3):
            arrived(("b0", d), ("b1", d))
        for kk in range(2):
            tb[kk, 0:HR] = pa0[kk, y] + rb0[0, kk] + rb0[1, kk] + rb0[2, kk]
            tb[kk, HR:ROWS] = pa1[2 * x + kk] + rb1[0, kk] + rb1[1, kk] + rb1[2, kk]
        for i in range(NZ):
            part = pl.ds(i * (ROWS // NZ), ROWS // NZ)
            copies["z_sum", i] = send(RS_Z + i, tb.at[1 - zl, part], rz.at[part], pair)

    below, above, far = 2 * turn(zh, -1) + c, 2 * turn(zh, 1) + c, 2 * turn(zh, 2) + c

    def w_on():
        arrived(("w_up", 0), ("w_up", 1))
        copies["w_up2"] = send(W_UP2, wb.at[below, 0:HB], wb.at[below, 0:HB], up)
        arrived(("w_down", 0), ("w_down", 1))
        copies["w_down2"] = send(W_DOWN2, wb.at[above, HB:B], wb.at[above, HB:B], down)

    def w_share():
        arrived(("w_up", 2), ("w_up", 3))
        copies["w_core_up"] = send(W_CORE_UP, wb.at[below], wb.at[below], core)
        arrived(("w_down", 2), ("w_down", 3))
        copies["w_core_down"] = send(W_CORE_DOWN, wb.at[above], wb.at[above], core)

    def frag_update():
        arrived(*[("z_sum", i) for i in range(NZ)])
        own_po.wait()
        own_pm.wait()
        average = (tb[zl] + rz[...]) / REPLICAS
        pseudo_grad = po[...] - average
        new_momentum = OUTER_MOMENTUM * pm[...] + pseudo_grad
        new_outer = po[...] - OUTER_RATE * (pseudo_grad + OUTER_MOMENTUM * new_momentum)
        mom_out[...] = new_momentum
        outer_out[...] = new_outer
        agb[2 * x + zl, y] = new_outer
        for i in range(NZ):
            part = agb.at[2 * x + zl, y, pl.ds(i * (ROWS // NZ), ROWS // NZ)]
            copies["z_gather", i] = send(AG_Z + i, part, part, pair)

    def frag_c():
        arrived(*[("z_gather", i) for i in range(NZ)])
        for d in (1, 2, 3):
            lower, upper = agb.at[pl.ds(2 * x, 2), y, 0:HR], agb.at[pl.ds(2 * x, 2), y, HR:ROWS]
            copies["c0", d] = send(AG_A0 + d - 1, lower, lower, at_x(d))
            copies["c1", d] = send(AG_A1 + d - 1, upper, upper, at_y(d))

    def frag_d():
        arrived(("c0", 1), ("c0", 2), ("c0", 3))
        for d in (1, 2, 3):
            lower = agb.at[:, y, 0:HR]
            copies["d0", d] = send(AG_B0 + d - 1, lower, lower, at_y(d))
        arrived(("c1", 1), ("c1", 2), ("c1", 3))
        for d in (1, 2, 3):
            upper = agb.at[pl.ds(2 * x, 2), :, HR:ROWS]
            copies["d1", d] = send(AG_B1 + d - 1, upper, upper, at_x(d))

    def frag_merge():
        for d in (1, 2, 3):
            arrived(("d0", d), ("d1", d))
        for k in range(32):
            block = MERGE_WEIGHT * slab[k // 4, k % 4].astype(F32) + (1.0 - MERGE_WEIGHT) * agb[k // 4, k % 4]
            local_out[:, k * LANES:(k + 1) * LANES] = block.astype(BF16)

    def project_near():
        arrived("w_core_up", "w_core_down")
        for s in (-1, 1):
            project(2 * turn(zh, s) + c)
            project(2 * turn(zh, s) + 1 - c)

    def w_far():
        arrived("w_up2")
        copies["w_far"] = send(W_CORE_FAR, wb.at[far, 0:HB], wb.at[far, 0:HB], core)
        arrived("w_down2")
        copies["w_far2"] = send(W_CORE_FAR2, wb.at[far, HB:B], wb.at[far, HB:B], core)

    def project_far():
        project(far)
        arrived("w_far", "w_far2")
        project(2 * turn(zh, 2) + 1 - c)
        proj_out[...] = acc[...].astype(BF16)

    def adam(half):
        tiles[1] = spread(rc[4 + half] * (1.0 / TOP))

        def body(at):
            rows_at = pl.ds(half * HB + at, 32)
            grad = g[0, rows_at] + unpacked(rg[4 + half, pl.ds(at, 32)]) * tiles[1]
            new_first = BETA_ONE * m1[rows_at] + (1.0 - BETA_ONE) * grad
            new_second = BETA_TWO * m2[rows_at] + (1.0 - BETA_TWO) * grad * grad
            weight = wb[f, rows_at].astype(F32)
            update = new_first / FIRST_FIX / (jnp.sqrt(new_second / SECOND_FIX) + EPSILON) + DECAY_RATE * weight
            first_out[rows_at] = new_first
            second_out[rows_at] = new_second
            neww_out[rows_at] = (weight - INNER_RATE * update).astype(BF16)
        chunks(body)

    def inner():
        own_m1.wait()
        own_m2.wait()
        arrived_g("g_up2")
        adam(0)
        arrived_g("g_down2")
        adam(1)

    own_w.wait()
    send_w(0, 1)
    load_slab()
    send_core()
    frag_send()
    send_w_core()
    grad_first()
    frag_a()
    grad_near()
    gradient(0)
    project(f, True)
    project_core()
    frag_b()
    send_w(2)
    frag_update()
    frag_c()
    send_w(3)
    grad_join()
    send_near()
    w_on()
    w_share()
    project_near()
    frag_d()
    grad_fold()
    frag_merge()
    inner()
    w_far()
    project_far()
    for copy in sent:
        copy.wait_send()


def shards(tokens, key_cotangent, key_weight, first_moment, second_moment, local_slab, outer_params, outer_momentum):
    out_shape = (
        jax.ShapeDtypeStruct((B, B), BF16),
        jax.ShapeDtypeStruct((B, B), BF16),
        jax.ShapeDtypeStruct((B, B), F32),
        jax.ShapeDtypeStruct((B, B), F32),
        jax.ShapeDtypeStruct((ROWS, LANES), F32),
        jax.ShapeDtypeStruct((ROWS, LANES), F32),
        jax.ShapeDtypeStruct((ROWS, 4096), BF16),
    )
    vmem = pltpu.VMEM
    results = pl.pallas_call(
        kernel,
        out_shape=tuple(pltpu.VMEM(o.shape, o.dtype) for o in out_shape),
        in_specs=[pl.BlockSpec(memory_space=pl.ANY)] * 8,
        out_specs=(pl.BlockSpec(memory_space=pltpu.VMEM),) * 7,
        scratch_shapes=[
            vmem((8, B, B), BF16),
            vmem((4, B, B), BF16),
            vmem((B, B), BF16),
            vmem((B, B), BF16),
            vmem((8, B, B), BF16),
            vmem((4, B, B), F32),
            vmem((6, HB, B), BF16),
            vmem((6, 8, LANES), F32),
            vmem((2, 32, B), F32),
            vmem((6, HB, B), BF16),
            vmem((6, 8, LANES), F32),
            vmem((B, B), F32),
            vmem((B, B), F32),
            vmem((8, 4, ROWS, LANES), BF16),
            vmem((3, 2, 4, HR, LANES), BF16),
            vmem((3, 8, HR, LANES), BF16),
            vmem((2, 4, HR, LANES), F32),
            vmem((8, HR, LANES), F32),
            vmem((3, 2, HR, LANES), F32),
            vmem((3, 2, HR, LANES), F32),
            vmem((2, ROWS, LANES), F32),
            vmem((ROWS, LANES), F32),
            vmem((ROWS, LANES), F32),
            vmem((ROWS, LANES), F32),
            vmem((8, 4, ROWS, LANES), F32),
            vmem((B, B), F32),
            pltpu.SemaphoreType.DMA((N_REMOTE,)),
            pltpu.SemaphoreType.DMA((N_REMOTE,)),
            pltpu.SemaphoreType.DMA((6,)),
            pltpu.SemaphoreType.DMA((8,)),
            pltpu.SemaphoreType.DMA((32,)),
        ],
        name="window",
        compiler_params=pltpu.CompilerParams(
            collective_id=0, has_side_effects=True, vmem_limit_bytes=40 << 20
        ),
    )(*[pltpu.with_memory_space_constraint(a, pltpu.HBM) for a in (tokens, key_cotangent, key_weight, first_moment, second_moment, local_slab, outer_params, outer_momentum)])

    def deliver(*refs):
        copies = [pltpu.make_async_copy(refs[i], refs[7 + i], refs[14].at[i]) for i in range(7)]
        for copy in copies:
            copy.start()
        for copy in copies:
            copy.wait()

    return pl.pallas_call(
        deliver,
        out_shape=out_shape,
        in_specs=[pl.BlockSpec(memory_space=pltpu.VMEM)] * 7,
        out_specs=(pl.BlockSpec(memory_space=pl.ANY),) * 7,
        scratch_shapes=[pltpu.SemaphoreType.DMA((7,))],
        name="deliver",
        compiler_params=pltpu.CompilerParams(vmem_limit_bytes=8 << 20),
    )(*results)


def solution(mesh):
    both = P(("replica", "fsdp"), None)
    cut = P("fsdp", "replica")
    return jax.shard_map(
        shards,
        mesh=mesh,
        in_specs=(both, both, both, both, both, both, cut, cut),
        out_specs=(both, both, both, both, cut, cut, both),
        check_vma=False,
    )
```
